256 devices in a mesh: prow: 16 (over y, x), pcol: 16 (over z, core).
Axes of the slice: x: 4, y: 4, z: 8, core: 2. Of those that a mesh axis runs over, the one named last changes fastest.
Arguments:
- matrix: bfloat16 [1, 8192, 1, 8192], P(None, 'prow', None, 'pcol'), may hold values from -8 to 300, as said below
Outputs:
- factored: bfloat16 [1, 8192, 1, 8192], P(None, 'prow', None, 'pcol')
The draws below stay inside these ranges and needn't reach their ends.
Inputs may be any that keep to these rules, and one draw needn't show every extreme that they name: `matrix`: every leading 512 x 512 diagonal block met by the steps has an LU factorization without pivoting, with pivots far from zero.
All inputs are finite; a program needn't handle non-finite values.
Results may differ from the reference program's by a relative error of at most 0.002.
Values may be sent and summed in bfloat16 or wider, within the bound.
A program may use at most 64 MiB of HBM per device.

```python
import math
import jax
import jax.numpy as jnp
from jax import lax

NB = 512
RB_DEV = 1
CB_DEV = 1
STEPS = 1
N_PROW = 16
N_PCOL = 16


def draw_matrix(key, part):
    rows = RB_DEV * N_PROW * NB
    cols = CB_DEV * N_PCOL * NB
    key_entries = jax.random.fold_in(key, 11)
    key_rows = jax.random.fold_in(key, 12)
    key_cols = jax.random.fold_in(key, 13)
    key_diag = jax.random.fold_in(key, 14)
    entries = jnp.clip(jax.random.normal(key_entries, (rows, cols), jnp.float32), -4.0, 4.0)
    low_scale = 0.7
    high_scale = 1.4
    row_scale = jnp.exp(jax.random.uniform(key_rows, (rows, 1), jnp.float32, math.log(low_scale), math.log(high_scale)))
    col_scale = jnp.exp(jax.random.uniform(key_cols, (1, cols), jnp.float32, math.log(low_scale), math.log(high_scale)))
    strength = jax.random.uniform(key_diag, (rows, 1), jnp.float32, 3.0, 5.0)
    on_diag = jnp.arange(rows)[:, None] == jnp.arange(cols)[None, :]
    diag_value = strength * math.sqrt(NB) * row_scale * col_scale
    values = jnp.where(on_diag, diag_value, entries * row_scale * col_scale)
    return values.astype(jnp.bfloat16).reshape(RB_DEV, N_PROW * NB, CB_DEV, N_PCOL * NB)


def setup_inputs(seed: int = 0) -> dict:
    key_list = jax.random.split(jax.random.key(seed), 2)
    matrix = draw_matrix(jax.random.fold_in(key_list[1], 71), 0)
    return {"matrix": matrix}


def lu_loop(block):
    size = block.shape[0]
    index = jnp.arange(size)

    def one_column(col, work):
        pivot = work[col, col]
        below = jnp.where(index > col, work[:, col] / pivot, jnp.zeros_like(work[:, col]))
        right = jnp.where(index > col, work[col, :], jnp.zeros_like(work[col, :]))
        work = work - below[:, None] * right[None, :]
        work = work.at[:, col].set(jnp.where(index > col, below, work[:, col]))
        return work
    return lax.fori_loop(0, size, one_column, block)

def factor_parts(block):
    packed = lu_loop(block)
    size = block.shape[0]
    ident = jnp.eye(size, dtype=packed.dtype)
    lower = jnp.tril(packed, -1) + ident
    upper = jnp.triu(packed)
    l_inverse = lax.linalg.triangular_solve(lower, ident, left_side=True, lower=True, unit_diagonal=True)
    u_inverse = lax.linalg.triangular_solve(upper, ident, left_side=True, lower=False)
    return (packed, l_inverse, u_inverse)

def reference(matrix):
    row_blocks, row_width, col_blocks, col_width = matrix.shape
    total_rows = row_blocks * row_width
    total_cols = col_blocks * col_width
    whole = matrix.reshape(total_rows, total_cols)
    for step in range(STEPS):
        low = step * NB
        high = low + NB
        diag = whole[low:high, low:high].astype(jnp.float32)
        packed, l_inverse, u_inverse = factor_parts(diag)
        l_panel = jnp.dot(whole[high:, low:high].astype(jnp.float32), u_inverse, precision=lax.Precision.HIGHEST).astype(jnp.bfloat16)
        u_panel = jnp.dot(l_inverse, whole[low:high, high:].astype(jnp.float32), precision=lax.Precision.HIGHEST).astype(jnp.bfloat16)
        whole = whole.at[low:high, low:high].set(packed.astype(jnp.bfloat16))
        whole = whole.at[high:, low:high].set(l_panel)
        whole = whole.at[low:high, high:].set(u_panel)
        u_wide = u_panel.astype(jnp.float32)
        count = total_rows // NB - step - 1

        def update_rows(blk, mat):
            start = high + blk * NB
            start = jnp.asarray(start).astype(jnp.int32)
            first = jnp.asarray(high).astype(jnp.int32)
            lead = jnp.asarray(low).astype(jnp.int32)
            target = lax.dynamic_slice(mat, (start, first), (NB, total_cols - high))
            left = lax.dynamic_slice(mat, (start, lead), (NB, NB)).astype(jnp.float32)
            change = jnp.dot(left, u_wide, precision=lax.Precision.HIGHEST)
            fresh = (target.astype(jnp.float32) - change).astype(mat.dtype)
            return lax.dynamic_update_slice(mat, fresh, (start, first))
        whole = lax.fori_loop(0, count, update_rows, whole)
    return whole.reshape(row_blocks, row_width, col_blocks, col_width)
```

```python
import functools

import jax
import jax.numpy as jnp
from jax import lax
from jax.experimental import pallas as pl
from jax.experimental.pallas import tpu as pltpu
from jax.sharding import PartitionSpec as P

F32 = jnp.float32
BF = jnp.bfloat16
NB = 512
HB = 256
TB = 128
MESH = pl.DeviceIdType.MESH


def split(x):
    hi = x.astype(BF)
    lo = (x - hi.astype(F32)).astype(BF)
    return hi, lo

def dot(a, b):
    return jnp.dot(a, b, preferred_element_type=F32)

def dot3s(a, b):
    ah, al = a; bh, bl = b
    return dot(jnp.concatenate([ah, al, ah], 1), jnp.concatenate([bh, bh, bl], 0))

def dot3(a, b):
    return dot3s(split(a), split(b))

def iotas(rows=8):
    return (lax.broadcasted_iota(jnp.int32, (rows, 128), 0), lax.broadcasted_iota(jnp.int32, (rows, 128), 1))

def leaf(block, base):
    sub, lane = iotas()
    other = 64 - base
    tiles = []
    for t in range(8):
        eye = jnp.where(lane == other + 8 * t + sub, 1.0, 0.0)
        keep = (lane >= base) & (lane < base + 64)
        tiles.append(jnp.where(keep, block[8 * t:8 * t + 8, :], eye))
    low = [None] * 8
    for g in range(8):
        c0 = base + 8 * g
        inside = (lane >= c0) & (lane < c0 + 8)
        grp = tiles[g]
        cols = [jnp.broadcast_to(grp[:, c0 + j:c0 + j + 1], (8, 128)) for j in range(8)]
        outer = {}
        for t in list(range(g + 1, 8)) + [8 + s for s in range(g)]:
            src = tiles[t] if t < 8 else low[t - 8]
            outer[t] = [jnp.broadcast_to(src[:, c0 + j:c0 + j + 1], (8, 128)) for j in range(8)]
        done = (lane >= base) & (lane < c0)
        held = grp
        grp = jnp.where(done, 0.0, grp)
        mult = jnp.zeros((8, 128), F32)
        v = jnp.where(inside, jnp.where(lane == c0 + sub, 1.0, 0.0), grp)
        scale = jnp.zeros((8, 128), F32)
        for j in range(8):
            piv = jnp.broadcast_to(cols[j][j:j + 1, :], (8, 128))
            rcp = 1.0 / piv
            m = jnp.where(sub == j, 0.0, cols[j] * rcp)
            for i in range(j + 1, 8):
                cols[i] = cols[i] - m * jnp.broadcast_to(cols[i][j:j + 1, :], (8, 128))
            mlow = jnp.where(sub > j, m, 0.0)
            grp = grp - mlow * jnp.broadcast_to(grp[j:j + 1, :], (8, 128))
            mult = jnp.where(lane == c0 + j, m, mult)
            mv = jnp.where(inside & (sub > j), 0.0, m)
            v = v - mv * jnp.broadcast_to(v[j:j + 1, :], (8, 128))
            scale = jnp.where(sub == j, rcp, scale)
        grp = jnp.where(inside & (lane < c0 + sub), mult, grp)
        tiles[g] = jnp.where(done, held, grp)
        v = v * scale
        v = jnp.where(inside, -v, v)
        rows = [jnp.broadcast_to(v[j:j + 1, :], (8, 128)) for j in range(8)]
        for t, cs in outer.items():
            src = tiles[t] if t < 8 else low[t - 8]
            p = [cs[j] * rows[j] for j in range(8)]
            tot = ((p[0] + p[1]) + (p[2] + p[3])) + ((p[4] + p[5]) + (p[6] + p[7]))
            new = jnp.where(inside, 0.0, src) - tot
            if t < 8:
                tiles[t] = new
            else:
                low[t - 8] = new
        low[g] = -v
    return jnp.concatenate(tiles, 0), jnp.concatenate(low, 0)

def lu128(blk):
    sub, lane = iotas(64)
    left = lane < 64
    z = jnp.zeros((64, 128), F32)
    top, bot = blk[:64], blk[64:]
    t0, b0 = leaf(top, 0)
    linv0 = jnp.where(left, 0.0, t0)
    uinv0 = jnp.where(left, b0, 0.0)
    u01 = jnp.where(left, 0.0, dot3(linv0, jnp.concatenate([z, top], 0)))
    l10 = dot3(jnp.where(left, bot, 0.0), jnp.concatenate([uinv0, z], 0))
    sch = bot - dot3(l10, jnp.concatenate([u01, z], 0))
    t1, b1 = leaf(sch, 64)
    linv0r = pltpu.roll(linv0, 64, 1)
    zl = dot3(l10, jnp.concatenate([linv0r, z], 0))
    zu = dot3(uinv0, jnp.concatenate([u01, z], 0))
    linv1 = jnp.where(left, t1, 0.0)
    uinv1 = jnp.where(left, 0.0, b1)
    linv10 = dot3(linv1, jnp.concatenate([zl, z], 0))
    uinv01 = dot3(zu, jnp.concatenate([z, uinv1], 0))
    packed = jnp.concatenate([jnp.where(left, t0, u01), jnp.where(left, l10, t1)], 0)
    linv = jnp.concatenate([linv0r, pltpu.roll(linv1, 64, 1) - linv10], 0)
    uinv = jnp.concatenate([uinv0 - uinv01, uinv1], 0)
    return packed, linv, uinv


def blk(i):
    return slice(TB * i, TB * (i + 1))


def later(i):
    return slice(TB * (i + 1), NB)


def pair_update(a_ref, li_ref, ui_ref, k):
    n = k + 1
    u = dot3(li_ref[k], a_ref[blk(k), blk(n)])
    l = dot3(a_ref[blk(n), blk(k)], ui_ref[k])
    a_ref[blk(k), blk(n)] = u
    a_ref[blk(n), blk(k)] = l
    a_ref[blk(n), blk(n)] = a_ref[blk(n), blk(n)] - dot3(l, u)


def half_update(a_ref, li_ref, ui_ref):
    rest = slice(HB, NB)
    u0 = dot3(li_ref[0], a_ref[blk(0), rest])
    l0 = dot3(a_ref[rest, blk(0)], ui_ref[0])
    u1 = dot3(li_ref[1], a_ref[blk(1), rest] - dot3(a_ref[blk(1), blk(0)], u0))
    l1 = dot3(a_ref[rest, blk(1)] - dot3(l0, a_ref[blk(0), blk(1)]), ui_ref[1])
    a_ref[blk(0), rest] = u0
    a_ref[blk(1), rest] = u1
    a_ref[rest, blk(0)] = l0
    a_ref[rest, blk(1)] = l1
    left = split(jnp.concatenate([l0, l1], 1))
    right = split(jnp.concatenate([u0, u1], 0))
    a_ref[rest, rest] = a_ref[rest, rest] - dot3s(left, right)


def panel_solve(a_ref, li_ref, ui_ref, q_ref, p_ref, ub_ref, lb_ref, j):
    u = dot3(li_ref[j], q_ref[blk(j), :])
    l = dot3(p_ref[:, blk(j)], ui_ref[j])
    ub_ref[blk(j), :] = u.astype(BF)
    lb_ref[:, blk(j)] = l.astype(BF)
    if j < 3:
        q_ref[later(j), :] = q_ref[later(j), :] - dot3(a_ref[later(j), blk(j)], u)
        p_ref[:, later(j)] = p_ref[:, later(j)] - dot3(l, a_ref[blk(j), later(j)])


def step_kernel(prows, pcols, remote, w_ref, o_ref, a_ref, q_ref, p_ref, li_ref, ui_ref, ub_ref, lb_ref,
                c_buf, d_buf, q_buf, p_buf, loc_sem, *sems):
    my_row = lax.axis_index("prow") if remote else 1
    my_col = lax.axis_index("pcol") if remote else 1
    hold = HB // prows
    q_hold = NB // prows
    p_hold = NB // pcols
    if remote:
        (q_send, q_recv, qs_send, qs_recv, p_send, p_recv, ps_send, ps_recv,
         c_send, c_recv, cz_send, cz_recv, ds_send, ds_recv, dz_send, dz_recv, da_send, da_recv) = sems

        def ring(axis, size, me, fn):
            def one(s, carry):
                fn(s, lax.rem(me + s, size), {axis: lax.rem(me + s, size)})
                return carry
            lax.fori_loop(1, size, one, 0)

        def rcopy(src, dst, ss, rs, dev):
            return pltpu.make_async_remote_copy(src_ref=src, dst_ref=dst, send_sem=ss, recv_sem=rs,
                                                device_id=dev, device_id_type=MESH)

        barrier = pltpu.get_barrier_semaphore()
        ring("prow", prows, my_row, lambda s, o, dev: pl.semaphore_signal(barrier, inc=1, device_id=dev, device_id_type=MESH))
        ring("pcol", pcols, my_col, lambda s, o, dev: pl.semaphore_signal(barrier, inc=1, device_id=dev, device_id_type=MESH))
        pl.semaphore_wait(barrier, prows + pcols - 2)

        def d_parts(ref, i):
            r = pl.ds(pl.multiple_of(i * hold, hold), hold)
            r2 = pl.ds(pl.multiple_of(HB + i * hold, hold), hold)
            return [ref.at[r, pl.ds(0, HB)], ref.at[r, pl.ds(HB, HB)], ref.at[r2, :]]

        def rows(ref, i, n):
            return ref.at[pl.ds(pl.multiple_of(i * n, n), n), :]

        corner = w_ref.at[pl.ds(0, TB), pl.ds(0, TB)]

        root = jnp.logical_and(my_row == 0, my_col == 0)

        @pl.when(root)
        def _():
            ring("prow", prows, my_row, lambda s, o, dev: rcopy(corner, c_buf, c_send.at[s], c_recv, dev).start())
            for part in range(3):
                ring("prow", prows, my_row, lambda s, o, dev: rcopy(
                    d_parts(w_ref, o)[part], d_parts(d_buf, o)[part], ds_send.at[part, s], ds_recv.at[part], dev).start())
            pltpu.make_async_copy(corner, c_buf, loc_sem.at[0]).start()
            for part in range(3):
                pltpu.make_async_copy(d_parts(w_ref, 0)[part], d_parts(d_buf, 0)[part], loc_sem.at[1 + part]).start()
            pltpu.make_async_copy(corner, c_buf, loc_sem.at[0]).wait()

        @pl.when(my_col == 0)
        def _():
            @pl.when(my_row != 0)
            def _():
                rcopy(corner, c_buf, c_send.at[0], c_recv, {"prow": 0}).wait_recv()
            ring("pcol", pcols, my_col, lambda s, o, dev: rcopy(c_buf, c_buf, cz_send.at[s], cz_recv, dev).start())
            for part in range(3):
                mine = d_parts(d_buf, my_row)[part]

                @pl.when(my_row == 0)
                def _():
                    pltpu.make_async_copy(d_parts(w_ref, 0)[part], mine, loc_sem.at[1 + part]).wait()

                @pl.when(my_row != 0)
                def _():
                    rcopy(mine, mine, ds_send.at[part, 0], ds_recv.at[part], {"prow": 0}).wait_recv()
                ring("pcol", pcols, my_col, lambda s, o, dev: rcopy(mine, mine, dz_send.at[part, s], dz_recv.at[part], dev).start())

        @pl.when(my_row == 0)
        def _():
            ring("prow", prows, my_row, lambda s, o, dev: rcopy(
                rows(w_ref, o, q_hold), rows(q_buf, o, q_hold), qs_send.at[s], qs_recv, dev).start())
            pltpu.make_async_copy(rows(w_ref, 0, q_hold), rows(q_buf, 0, q_hold), loc_sem.at[4]).start()

        @pl.when(my_col == 0)
        def _():
            ring("pcol", pcols, my_col, lambda s, o, dev: rcopy(
                rows(w_ref, o, p_hold), rows(p_buf, o, p_hold), ps_send.at[s], ps_recv, dev).start())
            pltpu.make_async_copy(rows(w_ref, 0, p_hold), rows(p_buf, 0, p_hold), loc_sem.at[5]).start()

        @pl.when(my_col != 0)
        def _():
            rcopy(c_buf, c_buf, cz_send.at[0], cz_recv, {"pcol": 0}).wait_recv()

    a_ref[0:TB, 0:TB] = c_buf[...].astype(F32)

    def pass_on_d():
        for part in range(3):
            mine = d_parts(d_buf, my_row)[part]

            @pl.when(my_col != 0)
            def _():
                rcopy(mine, mine, dz_send.at[part, 0], dz_recv.at[part], {"pcol": 0}).wait_recv()
            ring("prow", prows, my_row, lambda s, o, dev: rcopy(
                mine, mine, da_send.at[part, s], da_recv.at[part, my_row], dev).start())

    def pass_on_panels():
        mine_q = rows(q_buf, my_row, q_hold)
        mine_p = rows(p_buf, my_col, p_hold)

        @pl.when(my_row == 0)
        def _():
            pltpu.make_async_copy(rows(w_ref, 0, q_hold), mine_q, loc_sem.at[4]).wait()

        @pl.when(my_row != 0)
        def _():
            rcopy(mine_q, mine_q, qs_send.at[0], qs_recv, {"prow": 0}).wait_recv()

        @pl.when(my_col == 0)
        def _():
            pltpu.make_async_copy(rows(w_ref, 0, p_hold), mine_p, loc_sem.at[5]).wait()

        @pl.when(my_col != 0)
        def _():
            rcopy(mine_p, mine_p, ps_send.at[0], ps_recv, {"pcol": 0}).wait_recv()
        ring("prow", prows, my_row, lambda s, o, dev: rcopy(mine_q, mine_q, q_send.at[s], q_recv.at[my_row], dev).start())
        ring("pcol", pcols, my_col, lambda s, o, dev: rcopy(mine_p, mine_p, p_send.at[s], p_recv.at[my_col], dev).start())

    def get_d(part):
        ring("prow", prows, my_row, lambda s, o, dev: rcopy(
            d_parts(d_buf, o)[part], d_parts(d_buf, o)[part], da_send.at[part, s], da_recv.at[part, o], dev).wait_recv())

    def get_panels():
        ring("prow", prows, my_row, lambda s, o, dev: rcopy(
            rows(q_buf, o, q_hold), rows(q_buf, o, q_hold), q_send.at[s], q_recv.at[o], dev).wait_recv())
        ring("pcol", pcols, my_col, lambda s, o, dev: rcopy(
            rows(p_buf, o, p_hold), rows(p_buf, o, p_hold), p_send.at[s], p_recv.at[o], dev).wait_recv())

    def tile_step(k, carry):
        at = pl.ds(pl.multiple_of(k * TB, TB), TB)
        packed, linv, uinv = lu128(a_ref[at, at])
        a_ref[at, at] = packed
        li_ref[k] = linv
        ui_ref[k] = uinv

        @pl.when(k == 0)
        def _():
            if remote:
                pass_on_d()
                get_d(0)
            a_ref[0:TB, TB:HB] = d_buf[0:TB, TB:HB].astype(F32)
            a_ref[TB:HB, 0:HB] = d_buf[TB:HB, 0:HB].astype(F32)
            pair_update(a_ref, li_ref, ui_ref, 0)

        @pl.when(k == 1)
        def _():
            if remote:
                pass_on_panels()
                get_d(1)
                get_d(2)
            a_ref[0:HB, HB:NB] = d_buf[0:HB, HB:NB].astype(F32)
            a_ref[HB:NB, :] = d_buf[HB:NB, :].astype(F32)
            half_update(a_ref, li_ref, ui_ref)

        @pl.when(k == 2)
        def _():
            pair_update(a_ref, li_ref, ui_ref, 2)
            if remote:
                get_panels()
            q_ref[...] = q_buf[...].astype(F32)
            p_ref[...] = p_buf[...].astype(F32)
            for j in range(3):
                panel_solve(a_ref, li_ref, ui_ref, q_ref, p_ref, ub_ref, lb_ref, j)
        return carry

    lax.fori_loop(0, 4, tile_step, 0)
    panel_solve(a_ref, li_ref, ui_ref, q_ref, p_ref, ub_ref, lb_ref, 3)

    @pl.when(jnp.logical_and(my_row != 0, my_col != 0))
    def _():
        o_ref[...] = (w_ref[...].astype(F32) - dot(lb_ref[...], ub_ref[...])).astype(BF)

    @pl.when(jnp.logical_and(my_row == 0, my_col != 0))
    def _():
        o_ref[...] = ub_ref[...]

    @pl.when(jnp.logical_and(my_row != 0, my_col == 0))
    def _():
        o_ref[...] = lb_ref[...]

    @pl.when(jnp.logical_and(my_row == 0, my_col == 0))
    def _():
        o_ref[...] = a_ref[...].astype(BF)

    if remote:
        @pl.when(root)
        def _():
            ring("prow", prows, my_row, lambda s, o, dev: rcopy(corner, c_buf, c_send.at[s], c_recv, dev).wait_send())
            for part in range(3):
                ring("prow", prows, my_row, lambda s, o, dev: rcopy(
                    d_parts(w_ref, o)[part], d_parts(d_buf, o)[part], ds_send.at[part, s], ds_recv.at[part], dev).wait_send())

        @pl.when(my_col == 0)
        def _():
            ring("pcol", pcols, my_col, lambda s, o, dev: rcopy(c_buf, c_buf, cz_send.at[s], cz_recv, dev).wait_send())
            for part in range(3):
                mine = d_parts(d_buf, my_row)[part]
                ring("pcol", pcols, my_col, lambda s, o, dev: rcopy(mine, mine, dz_send.at[part, s], dz_recv.at[part], dev).wait_send())
            ring("pcol", pcols, my_col, lambda s, o, dev: rcopy(
                rows(w_ref, o, p_hold), rows(p_buf, o, p_hold), ps_send.at[s], ps_recv, dev).wait_send())

        @pl.when(my_row == 0)
        def _():
            ring("prow", prows, my_row, lambda s, o, dev: rcopy(
                rows(w_ref, o, q_hold), rows(q_buf, o, q_hold), qs_send.at[s], qs_recv, dev).wait_send())
        for part in range(3):
            mine = d_parts(d_buf, my_row)[part]
            ring("prow", prows, my_row, lambda s, o, dev: rcopy(
                mine, mine, da_send.at[part, s], da_recv.at[part, my_row], dev).wait_send())
        mine_q = rows(q_buf, my_row, q_hold)
        mine_p = rows(p_buf, my_col, p_hold)
        ring("prow", prows, my_row, lambda s, o, dev: rcopy(mine_q, mine_q, q_send.at[s], q_recv.at[my_row], dev).wait_send())
        ring("pcol", pcols, my_col, lambda s, o, dev: rcopy(mine_p, mine_p, p_send.at[s], p_recv.at[my_col], dev).wait_send())


def per_device(matrix):
    prows, pcols = lax.axis_size("prow"), lax.axis_size("pcol")
    dma = pltpu.SemaphoreType.DMA
    out = pl.pallas_call(
        functools.partial(step_kernel, prows, pcols, True),
        out_shape=jax.ShapeDtypeStruct((NB, NB), BF),
        in_specs=[pl.BlockSpec(memory_space=pltpu.VMEM)],
        out_specs=pl.BlockSpec(memory_space=pltpu.VMEM),
        scratch_shapes=[
            pltpu.VMEM((NB, NB), F32), pltpu.VMEM((NB, NB), F32), pltpu.VMEM((NB, NB), F32),
            pltpu.VMEM((4, TB, TB), F32), pltpu.VMEM((4, TB, TB), F32),
            pltpu.VMEM((NB, NB), BF), pltpu.VMEM((NB, NB), BF),
            pltpu.VMEM((TB, TB), BF), pltpu.VMEM((NB, NB), BF), pltpu.VMEM((NB, NB), BF), pltpu.VMEM((NB, NB), BF),
            dma((6,)),
            dma((prows,)), dma((prows,)), dma((prows,)), dma,
            dma((pcols,)), dma((pcols,)), dma((pcols,)), dma,
            dma((prows,)), dma, dma((pcols,)), dma,
            dma((3, prows)), dma((3,)), dma((3, pcols)), dma((3,)), dma((3, prows)), dma((3, prows)),
        ],
        compiler_params=pltpu.CompilerParams(collective_id=0, has_side_effects=True),
    )(matrix.reshape(NB, NB))
    return out.reshape(matrix.shape)


def solution(mesh):
    placed = P(None, "prow", None, "pcol")
    return jax.shard_map(per_device, mesh=mesh, in_specs=(placed,), out_specs=placed, check_vma=False)
```

```python
import functools

import jax
import jax.numpy as jnp
from jax import lax
from jax.experimental import pallas as pl
from jax.experimental.pallas import tpu as pltpu
from jax.sharding import PartitionSpec as P

F32 = jnp.float32
BF = jnp.bfloat16
NB = 512
HB = 256
TB = 128
MESH = pl.DeviceIdType.MESH


def split(x):
    hi = x.astype(BF)
    lo = (x - hi.astype(F32)).astype(BF)
    return hi, lo

def dot(a, b):
    return jnp.dot(a, b, preferred_element_type=F32)

def dot3s(a, b):
    ah, al = a; bh, bl = b
    return dot(jnp.concatenate([ah, al, ah], 1), jnp.concatenate([bh, bh, bl], 0))

def dot3(a, b):
    return dot3s(split(a), split(b))

def iotas(rows=8):
    return (lax.broadcasted_iota(jnp.int32, (rows, 128), 0), lax.broadcasted_iota(jnp.int32, (rows, 128), 1))

def leaf(block, base):
    sub, lane = iotas()
    other = 64 - base
    tiles = []
    for t in range(8):
        eye = jnp.where(lane == other + 8 * t + sub, 1.0, 0.0)
        keep = (lane >= base) & (lane < base + 64)
        tiles.append(jnp.where(keep, block[8 * t:8 * t + 8, :], eye))
    low = [None] * 8
    for g in range(8):
        c0 = base + 8 * g
        inside = (lane >= c0) & (lane < c0 + 8)
        grp = tiles[g]
        cols = [jnp.broadcast_to(grp[:, c0 + j:c0 + j + 1], (8, 128)) for j in range(8)]
        outer = {}
        for t in list(range(g + 1, 8)) + [8 + s for s in range(g)]:
            src = tiles[t] if t < 8 else low[t - 8]
            outer[t] = [jnp.broadcast_to(src[:, c0 + j:c0 + j + 1], (8, 128)) for j in range(8)]
        done = (lane >= base) & (lane < c0)
        held = grp
        grp = jnp.where(done, 0.0, grp)
        mult = jnp.zeros((8, 128), F32)
        v = jnp.where(inside, jnp.where(lane == c0 + sub, 1.0, 0.0), grp)
        scale = jnp.zeros((8, 128), F32)
        for j in range(8):
            piv = jnp.broadcast_to(cols[j][j:j + 1, :], (8, 128))
            rcp = 1.0 / piv
            m = jnp.where(sub == j, 0.0, cols[j] * rcp)
            for i in range(j + 1, 8):
                cols[i] = cols[i] - m * jnp.broadcast_to(cols[i][j:j + 1, :], (8, 128))
            mlow = jnp.where(sub > j, m, 0.0)
            grp = grp - mlow * jnp.broadcast_to(grp[j:j + 1, :], (8, 128))
            mult = jnp.where(lane == c0 + j, m, mult)
            mv = jnp.where(inside & (sub > j), 0.0, m)
            v = v - mv * jnp.broadcast_to(v[j:j + 1, :], (8, 128))
            scale = jnp.where(sub == j, rcp, scale)
        grp = jnp.where(inside & (lane < c0 + sub), mult, grp)
        tiles[g] = jnp.where(done, held, grp)
        v = v * scale
        v = jnp.where(inside, -v, v)
        rows = [jnp.broadcast_to(v[j:j + 1, :], (8, 128)) for j in range(8)]
        for t, cs in outer.items():
            src = tiles[t] if t < 8 else low[t - 8]
            p = [cs[j] * rows[j] for j in range(8)]
            tot = ((p[0] + p[1]) + (p[2] + p[3])) + ((p[4] + p[5]) + (p[6] + p[7]))
            new = jnp.where(inside, 0.0, src) - tot
            if t < 8:
                tiles[t] = new
            else:
                low[t - 8] = new
        low[g] = -v
    return jnp.concatenate(tiles, 0), jnp.concatenate(low, 0)


def second_half(t0, b0, top, bot):
    _, lane = iotas(64)
    left = lane < 64
    z = jnp.zeros((64, 128), F32)
    linv0 = jnp.where(left, 0.0, t0)
    uinv0 = jnp.where(left, b0, 0.0)
    u01 = jnp.where(left, 0.0, dot3(linv0, jnp.concatenate([z, top], 0)))
    l10 = dot3(jnp.where(left, bot, 0.0), jnp.concatenate([uinv0, z], 0))
    sch = bot - dot3(l10, jnp.concatenate([u01, z], 0))
    t1, b1 = leaf(sch, 64)
    linv0r = pltpu.roll(linv0, 64, 1)
    zl = dot3(l10, jnp.concatenate([linv0r, z], 0))
    zu = dot3(uinv0, jnp.concatenate([u01, z], 0))
    linv1 = jnp.where(left, t1, 0.0)
    uinv1 = jnp.where(left, 0.0, b1)
    linv10 = dot3(linv1, jnp.concatenate([zl, z], 0))
    uinv01 = dot3(zu, jnp.concatenate([z, uinv1], 0))
    packed = jnp.concatenate([jnp.where(left, t0, u01), jnp.where(left, l10, t1)], 0)
    linv = jnp.concatenate([linv0r, pltpu.roll(linv1, 64, 1) - linv10], 0)
    uinv = jnp.concatenate([uinv0 - uinv01, uinv1], 0)
    return packed, linv, uinv


def blk(i):
    return slice(TB * i, TB * (i + 1))


def later(i):
    return slice(TB * (i + 1), NB)


def pair_update(a_ref, li_ref, ui_ref, k):
    n = k + 1
    u = dot3(li_ref[k], a_ref[blk(k), blk(n)])
    l = dot3(a_ref[blk(n), blk(k)], ui_ref[k])
    a_ref[blk(k), blk(n)] = u
    a_ref[blk(n), blk(k)] = l
    a_ref[blk(n), blk(n)] = a_ref[blk(n), blk(n)] - dot3(l, u)


def half_update(a_ref, li_ref, ui_ref):
    rest = slice(HB, NB)
    u0 = dot3(li_ref[0], a_ref[blk(0), rest])
    l0 = dot3(a_ref[rest, blk(0)], ui_ref[0])
    u1 = dot3(li_ref[1], a_ref[blk(1), rest] - dot3(a_ref[blk(1), blk(0)], u0))
    l1 = dot3(a_ref[rest, blk(1)] - dot3(l0, a_ref[blk(0), blk(1)]), ui_ref[1])
    a_ref[blk(0), rest] = u0
    a_ref[blk(1), rest] = u1
    a_ref[rest, blk(0)] = l0
    a_ref[rest, blk(1)] = l1
    left = split(jnp.concatenate([l0, l1], 1))
    right = split(jnp.concatenate([u0, u1], 0))
    a_ref[rest, rest] = a_ref[rest, rest] - dot3s(left, right)


def solve_u(a_ref, li_ref, q_ref, ub_ref, j):
    u = dot3(li_ref[j], q_ref[blk(j), :])
    ub_ref[blk(j), :] = u.astype(BF)
    if j < 3:
        q_ref[later(j), :] = q_ref[later(j), :] - dot3(a_ref[later(j), blk(j)], u)


def solve_l(a_ref, ui_ref, p_ref, lb_ref, j):
    l = dot3(p_ref[:, blk(j)], ui_ref[j])
    lb_ref[:, blk(j)] = l.astype(BF)
    if j < 3:
        p_ref[:, later(j)] = p_ref[:, later(j)] - dot3(l, a_ref[blk(j), later(j)])


def rcopy(src, dst, ss, rs, dev):
    return pltpu.make_async_remote_copy(src_ref=src, dst_ref=dst, send_sem=ss, recv_sem=rs,
                                        device_id=dev, device_id_type=MESH)


def each(lo, hi, fn):
    def one(s, carry):
        fn(s)
        return carry
    lax.fori_loop(lo, hi, one, 0)


class Moves:
    def __init__(self, prows, pcols, w_ref, c_buf, d_buf, q_buf, p_buf, loc_sem, sems):
        self.prows, self.pcols = prows, pcols
        self.row, self.col = lax.axis_index("prow"), lax.axis_index("pcol")
        self.core = lax.rem(self.col, 2)
        self.w, self.c, self.d, self.q, self.p = w_ref, c_buf, d_buf, q_buf, p_buf
        self.loc = loc_sem
        (self.c_send, self.c_recv, self.cz_send, self.cz_recv,
         self.ds_send, self.ds_recv, self.dz_send, self.dz_recv, self.da_send, self.da_recv,
         self.qs_send, self.qs_recv, self.qa_send, self.qa_recv,
         self.ps_send, self.ps_recv, self.pa_send, self.pa_recv, self.px_send, self.px_recv) = sems
        self.root = jnp.logical_and(self.row == 0, self.col == 0)
        self.passer = self.col == jnp.where(self.row == 0, 1, 0)
        self.pass_hi = jnp.where(self.row == 0, pcols - 1, pcols)
        self.has_q = self.col != 0
        self.has_p = self.row != 0

    def up(self, s):
        return lax.rem(self.row + s, self.prows)

    def along(self, s):
        return lax.rem(self.col + s, self.pcols)

    def same_core(self, s):
        return lax.rem(self.col + 2 * s, self.pcols)

    def ready(self):
        barrier = pltpu.get_barrier_semaphore()

        def tell(dev):
            pl.semaphore_signal(barrier, inc=1, device_id=dev, device_id_type=MESH)
        each(1, self.prows, lambda s: tell({"prow": self.up(s)}))

        @pl.when(self.has_p)
        def _():
            each(1, self.pcols, lambda s: tell({"pcol": self.along(s)}))

        @pl.when(jnp.logical_and(self.row == 0, self.col == 1))
        def _():
            tell({"pcol": 0})

        @pl.when(jnp.logical_and(self.row == 0, self.col > 1))
        def _():
            tell({"pcol": 1})
        zero_row = jnp.where(self.col == 0, 1, jnp.where(self.col == 1, self.pcols - 2, 0))
        pl.semaphore_wait(barrier, self.prows - 1 + jnp.where(self.has_p, self.pcols - 1, zero_row))

    def corner(self, ref, half):
        return ref.at[pl.ds(64 * half, 64), pl.ds(0, TB)]

    def part(self, ref, i, part):
        n = HB // self.prows
        top = pl.ds(pl.multiple_of(i * n, n), n)
        low = pl.ds(pl.multiple_of(HB + i * n, n), n)
        return [ref.at[top, pl.ds(0, HB)], ref.at[top, pl.ds(HB, HB)], ref.at[low, :]][part]

    def corner_out(self, half, s):
        return rcopy(self.corner(self.w, half), self.corner(self.c, half), self.c_send.at[half, s], self.c_recv.at[half],
                     {"prow": self.up(s)})

    def corner_side(self, half):
        return rcopy(self.corner(self.w, half), self.corner(self.c, half), self.cz_send.at[half, 0], self.cz_recv.at[half],
                     {"pcol": 1})

    def corner_on(self, half, s):
        piece = self.corner(self.c, half)
        return rcopy(piece, piece, self.cz_send.at[half, s], self.cz_recv.at[half], {"pcol": self.along(s)})

    def d_out(self, part, s):
        return rcopy(self.part(self.w, self.up(s), part), self.part(self.d, self.up(s), part),
                     self.ds_send.at[part, s], self.ds_recv.at[part], {"prow": self.up(s)})

    def d_side(self, part):
        return rcopy(self.part(self.w, 0, part), self.part(self.d, 0, part),
                     self.dz_send.at[part, 0], self.dz_recv.at[part], {"pcol": 1})

    def d_on(self, part, s):
        piece = self.part(self.d, self.row, part)
        return rcopy(piece, piece, self.dz_send.at[part, s], self.dz_recv.at[part], {"pcol": self.along(s)})

    def d_share(self, part, s):
        piece = self.part(self.d, self.row, part)
        return rcopy(piece, piece, self.da_send.at[part, s], self.da_recv.at[part, self.row], {"prow": self.up(s)})

    def d_from(self, part, s):
        o = self.up(s)
        piece = self.part(self.d, o, part)
        return rcopy(piece, piece, self.da_send.at[part, s], self.da_recv.at[part, o], {"prow": o})

    def own(self, i):
        if i < 2:
            return pltpu.make_async_copy(self.corner(self.w, i), self.corner(self.c, i), self.loc.at[i])
        if i < 5:
            return pltpu.make_async_copy(self.part(self.w, 0, i - 2), self.part(self.d, 0, i - 2), self.loc.at[i])
        if i == 5:
            return pltpu.make_async_copy(self.q_piece(self.w, 0), self.q_piece(self.q, 0), self.loc.at[i])
        return pltpu.make_async_copy(self.p_piece(self.w, 0), self.p_piece(self.p, 0), self.loc.at[i])

    def q_piece(self, ref, i):
        n = NB // self.prows
        return ref.at[pl.ds(pl.multiple_of(i * n, n), n), :]

    def q_out(self, s):
        o = self.up(s)
        return rcopy(self.q_piece(self.w, o), self.q_piece(self.q, o), self.qs_send.at[s], self.qs_recv, {"prow": o})

    def q_share(self, s):
        piece = self.q_piece(self.q, self.row)
        return rcopy(piece, piece, self.qa_send.at[s], self.qa_recv.at[self.row], {"prow": self.up(s)})

    def q_from(self, s):
        o = self.up(s)
        piece = self.q_piece(self.q, o)
        return rcopy(piece, piece, self.qa_send.at[s], self.qa_recv.at[o], {"prow": o})

    def p_piece(self, ref, c):
        n = NB // self.pcols
        at = lax.rem(c, 2) * HB + (c // 2) * n
        return ref.at[pl.ds(pl.multiple_of(at, n), n), :]

    def p_half(self, h):
        return self.p.at[pl.ds(pl.multiple_of(h * HB, HB), HB), :]

    def p_out(self, s):
        o = self.along(s)
        return rcopy(self.p_piece(self.w, o), self.p_piece(self.p, o), self.ps_send.at[s], self.ps_recv, {"pcol": o})

    def p_share(self, s):
        piece = self.p_piece(self.p, self.col)
        return rcopy(piece, piece, self.pa_send.at[s], self.pa_recv.at[self.col // 2], {"pcol": self.same_core(s)})

    def p_from(self, s):
        o = self.same_core(s)
        piece = self.p_piece(self.p, o)
        return rcopy(piece, piece, self.pa_send.at[s], self.pa_recv.at[o // 2], {"pcol": o})

    def p_swap(self):
        mine = self.p_half(self.core)
        return rcopy(mine, mine, self.px_send, self.px_recv, {"pcol": self.col + 1 - 2 * self.core})

    def p_swapped(self):
        other = self.p_half(1 - self.core)
        return rcopy(other, other, self.px_send, self.px_recv, {"pcol": self.col + 1 - 2 * self.core})

    def start(self):
        self.ready()

        @pl.when(self.root)
        def _():
            for half in range(2):
                each(1, self.prows, lambda s: self.corner_out(half, s).start())
                self.corner_side(half).start()
                self.own(half).start()
            for part in range(3):
                each(1, self.prows, lambda s: self.d_out(part, s).start())
                self.d_side(part).start()
                self.own(2 + part).start()

        @pl.when(jnp.logical_and(self.row == 0, self.col > 1))
        def _():
            self.send_q()

        @pl.when(self.passer)
        def _():
            for half in range(2):
                @pl.when(self.has_p)
                def _():
                    self.corner_out(half, 0).wait_recv()

                @pl.when(jnp.logical_not(self.has_p))
                def _():
                    self.corner_side(half).wait_recv()
                each(1, self.pass_hi, lambda s: self.corner_on(half, s).start())
            for part in range(3):
                @pl.when(self.has_p)
                def _():
                    self.d_out(part, 0).wait_recv()

                @pl.when(jnp.logical_not(self.has_p))
                def _():
                    self.d_side(part).wait_recv()
                each(1, self.pass_hi, lambda s: self.d_on(part, s).start())

            @pl.when(self.has_p)
            def _():
                each(1, self.pcols, lambda s: self.p_out(s).start())
                self.own(6).start()

            @pl.when(jnp.logical_not(self.has_p))
            def _():
                self.send_q()

    def send_q(self):
        each(1, self.prows, lambda s: self.q_out(s).start())
        self.own(5).start()

    def wait_corner(self, half):
        @pl.when(self.root)
        def _():
            self.own(half).wait()

        @pl.when(jnp.logical_not(jnp.logical_or(self.root, self.passer)))
        def _():
            self.corner_on(half, 0).wait_recv()

    def share_d(self, parts):
        for part in parts:
            @pl.when(self.root)
            def _():
                self.own(2 + part).wait()

            @pl.when(jnp.logical_not(jnp.logical_or(self.root, self.passer)))
            def _():
                self.d_on(part, 0).wait_recv()
            each(1, self.prows, lambda s: self.d_share(part, s).start())

    def get_d(self, part):
        each(1, self.prows, lambda s: self.d_from(part, s).wait_recv())

    def share_q(self):
        @pl.when(self.has_q)
        def _():
            @pl.when(self.row == 0)
            def _():
                self.own(5).wait()

            @pl.when(self.row != 0)
            def _():
                self.q_out(0).wait_recv()
            each(1, self.prows, lambda s: self.q_share(s).start())

    def get_q(self):
        each(1, self.prows, lambda s: self.q_from(s).wait_recv())

    def share_p(self):
        @pl.when(self.has_p)
        def _():
            @pl.when(self.col == 0)
            def _():
                self.own(6).wait()

            @pl.when(self.col != 0)
            def _():
                self.p_out(0).wait_recv()
            each(1, self.pcols // 2, lambda s: self.p_share(s).start())

    def swap_p(self):
        @pl.when(self.has_p)
        def _():
            each(1, self.pcols // 2, lambda s: self.p_from(s).wait_recv())
            self.p_swap().start()

    def get_p(self):
        self.p_swapped().wait_recv()

    def finish(self):
        @pl.when(self.root)
        def _():
            for half in range(2):
                each(1, self.prows, lambda s: self.corner_out(half, s).wait_send())
                self.corner_side(half).wait_send()
            for part in range(3):
                each(1, self.prows, lambda s: self.d_out(part, s).wait_send())
                self.d_side(part).wait_send()

        @pl.when(self.passer)
        def _():
            for half in range(2):
                each(1, self.pass_hi, lambda s: self.corner_on(half, s).wait_send())
            for part in range(3):
                each(1, self.pass_hi, lambda s: self.d_on(part, s).wait_send())

            @pl.when(self.has_p)
            def _():
                each(1, self.pcols, lambda s: self.p_out(s).wait_send())
        for part in range(3):
            each(1, self.prows, lambda s: self.d_share(part, s).wait_send())

        @pl.when(self.has_q)
        def _():
            @pl.when(self.row == 0)
            def _():
                each(1, self.prows, lambda s: self.q_out(s).wait_send())
            each(1, self.prows, lambda s: self.q_share(s).wait_send())

        @pl.when(self.has_p)
        def _():
            each(1, self.pcols // 2, lambda s: self.p_share(s).wait_send())
            self.p_swap().wait_send()


def step_kernel(prows, pcols, w_ref, o_ref, a_ref, q_ref, p_ref, li_ref, ui_ref, ub_ref, lb_ref,
                c_buf, d_buf, q_buf, p_buf, loc_sem, *sems):
    mv = Moves(prows, pcols, w_ref, c_buf, d_buf, q_buf, p_buf, loc_sem, sems)
    mv.start()
    mv.wait_corner(0)
    a_ref[0:64, 0:TB] = c_buf[0:64, :].astype(F32)

    def tile_step(k, carry):
        at = pl.ds(pl.multiple_of(k * TB, TB), TB)
        upper = pl.ds(pl.multiple_of(k * TB, 64), 64)
        lower = pl.ds(pl.multiple_of(k * TB + 64, 64), 64)
        top = a_ref[upper, at]
        t0, b0 = leaf(top, 0)

        @pl.when(k == 0)
        def _():
            mv.wait_corner(1)
            a_ref[64:TB, 0:TB] = c_buf[64:TB, :].astype(F32)
            mv.share_d([0, 1, 2])

        @pl.when(k == 1)
        def _():
            mv.share_q()

        @pl.when(k == 3)
        def _():
            @pl.when(mv.has_q)
            def _():
                mv.get_q()
                q_ref[...] = q_buf[...].astype(F32)
                for j in range(3):
                    solve_u(a_ref, li_ref, q_ref, ub_ref, j)

            @pl.when(mv.has_p)
            def _():
                mv.get_p()
                p_ref[...] = p_buf[...].astype(F32)
                for j in range(3):
                    solve_l(a_ref, ui_ref, p_ref, lb_ref, j)

        packed, linv, uinv = second_half(t0, b0, top, a_ref[lower, at])
        a_ref[at, at] = packed
        li_ref[k] = linv
        ui_ref[k] = uinv

        @pl.when(k == 0)
        def _():
            mv.share_p()
            mv.get_d(0)
            a_ref[0:TB, TB:HB] = d_buf[0:TB, TB:HB].astype(F32)
            a_ref[TB:HB, 0:HB] = d_buf[TB:HB, 0:HB].astype(F32)
            pair_update(a_ref, li_ref, ui_ref, 0)

        @pl.when(k == 1)
        def _():
            mv.get_d(1)
            mv.get_d(2)
            a_ref[0:HB, HB:NB] = d_buf[0:HB, HB:NB].astype(F32)
            a_ref[HB:NB, :] = d_buf[HB:NB, :].astype(F32)
            half_update(a_ref, li_ref, ui_ref)

        @pl.when(k == 2)
        def _():
            pair_update(a_ref, li_ref, ui_ref, 2)
            mv.swap_p()
        return carry

    lax.fori_loop(0, 4, tile_step, 0)

    @pl.when(mv.has_q)
    def _():
        solve_u(a_ref, li_ref, q_ref, ub_ref, 3)

    @pl.when(mv.has_p)
    def _():
        solve_l(a_ref, ui_ref, p_ref, lb_ref, 3)

    @pl.when(jnp.logical_and(mv.has_p, mv.has_q))
    def _():
        o_ref[...] = (w_ref[...].astype(F32) - dot(lb_ref[...], ub_ref[...])).astype(BF)

    @pl.when(jnp.logical_and(jnp.logical_not(mv.has_p), mv.has_q))
    def _():
        o_ref[...] = ub_ref[...]

    @pl.when(jnp.logical_and(mv.has_p, jnp.logical_not(mv.has_q)))
    def _():
        o_ref[...] = lb_ref[...]

    @pl.when(mv.root)
    def _():
        o_ref[...] = a_ref[...].astype(BF)

    mv.finish()


def per_device(matrix):
    prows, pcols = lax.axis_size("prow"), lax.axis_size("pcol")
    dma = pltpu.SemaphoreType.DMA
    out = pl.pallas_call(
        functools.partial(step_kernel, prows, pcols),
        out_shape=jax.ShapeDtypeStruct((NB, NB), BF),
        in_specs=[pl.BlockSpec(memory_space=pltpu.VMEM)],
        out_specs=pl.BlockSpec(memory_space=pltpu.VMEM),
        scratch_shapes=[
            pltpu.VMEM((NB, NB), F32), pltpu.VMEM((NB, NB), F32), pltpu.VMEM((NB, NB), F32),
            pltpu.VMEM((4, TB, TB), F32), pltpu.VMEM((4, TB, TB), F32),
            pltpu.VMEM((NB, NB), BF), pltpu.VMEM((NB, NB), BF),
            pltpu.VMEM((TB, TB), BF), pltpu.VMEM((NB, NB), BF), pltpu.VMEM((NB, NB), BF), pltpu.VMEM((NB, NB), BF),
            dma((7,)),
            dma((2, prows)), dma((2,)), dma((2, pcols)), dma((2,)),
            dma((3, prows)), dma((3,)), dma((3, pcols)), dma((3,)), dma((3, prows)), dma((3, prows)),
            dma((prows,)), dma, dma((prows,)), dma((prows,)),
            dma((pcols,)), dma, dma((pcols // 2,)), dma((pcols // 2,)), dma, dma,
        ],
        compiler_params=pltpu.CompilerParams(collective_id=0, has_side_effects=True),
    )(matrix.reshape(NB, NB))
    return out.reshape(matrix.shape)


def solution(mesh):
    placed = P(None, "prow", None, "pcol")
    return jax.shard_map(per_device, mesh=mesh, in_specs=(placed,), out_specs=placed, check_vma=False)
```

```python
import functools

import jax
import jax.numpy as jnp
from jax import lax
from jax.experimental import pallas as pl
from jax.experimental.pallas import tpu as pltpu
from jax.sharding import PartitionSpec as P

F32 = jnp.float32
BF = jnp.bfloat16
NB = 512
HB = 256
TB = 128
PARTS = 5
OWN_Q, OWN_P = 2 + PARTS, 3 + PARTS
MESH = pl.DeviceIdType.MESH


def split(x):
    hi = x.astype(BF)
    lo = (x - hi.astype(F32)).astype(BF)
    return hi, lo

def dot(a, b):
    return jnp.dot(a, b, preferred_element_type=F32)

def dot3s(a, b):
    ah, al = a; bh, bl = b
    return dot(jnp.concatenate([ah, al, ah], 1), jnp.concatenate([bh, bh, bl], 0))

def dot3(a, b):
    return dot3s(split(a), split(b))

def iotas(rows=8):
    return (lax.broadcasted_iota(jnp.int32, (rows, 128), 0), lax.broadcasted_iota(jnp.int32, (rows, 128), 1))

def leaf(block, base):
    sub, lane = iotas()
    other = 64 - base
    tiles = []
    for t in range(8):
        eye = jnp.where(lane == other + 8 * t + sub, 1.0, 0.0)
        keep = (lane >= base) & (lane < base + 64)
        tiles.append(jnp.where(keep, block[8 * t:8 * t + 8, :], eye))
    low = [None] * 8
    for g in range(8):
        c0 = base + 8 * g
        inside = (lane >= c0) & (lane < c0 + 8)
        grp = tiles[g]
        cols = [jnp.broadcast_to(grp[:, c0 + j:c0 + j + 1], (8, 128)) for j in range(8)]
        outer = {}
        for t in list(range(g + 1, 8)) + [8 + s for s in range(g)]:
            src = tiles[t] if t < 8 else low[t - 8]
            outer[t] = [jnp.broadcast_to(src[:, c0 + j:c0 + j + 1], (8, 128)) for j in range(8)]
        done = (lane >= base) & (lane < c0)
        held = grp
        grp = jnp.where(done, 0.0, grp)
        mult = jnp.zeros((8, 128), F32)
        v = jnp.where(inside, jnp.where(lane == c0 + sub, 1.0, 0.0), grp)
        scale = jnp.zeros((8, 128), F32)
        for j in range(8):
            piv = jnp.broadcast_to(cols[j][j:j + 1, :], (8, 128))
            rcp = 1.0 / piv
            m = jnp.where(sub == j, 0.0, cols[j] * rcp)
            for i in range(j + 1, 8):
                cols[i] = cols[i] - m * jnp.broadcast_to(cols[i][j:j + 1, :], (8, 128))
            mlow = jnp.where(sub > j, m, 0.0)
            grp = grp - mlow * jnp.broadcast_to(grp[j:j + 1, :], (8, 128))
            mult = jnp.where(lane == c0 + j, m, mult)
            mv = jnp.where(inside & (sub > j), 0.0, m)
            v = v - mv * jnp.broadcast_to(v[j:j + 1, :], (8, 128))
            scale = jnp.where(sub == j, rcp, scale)
        grp = jnp.where(inside & (lane < c0 + sub), mult, grp)
        tiles[g] = jnp.where(done, held, grp)
        v = v * scale
        v = jnp.where(inside, -v, v)
        rows = [jnp.broadcast_to(v[j:j + 1, :], (8, 128)) for j in range(8)]
        for t, cs in outer.items():
            src = tiles[t] if t < 8 else low[t - 8]
            p = [cs[j] * rows[j] for j in range(8)]
            tot = ((p[0] + p[1]) + (p[2] + p[3])) + ((p[4] + p[5]) + (p[6] + p[7]))
            new = jnp.where(inside, 0.0, src) - tot
            if t < 8:
                tiles[t] = new
            else:
                low[t - 8] = new
        low[g] = -v
    return jnp.concatenate(tiles, 0), jnp.concatenate(low, 0)


def second_half(t0, b0, top, bot):
    _, lane = iotas(64)
    left = lane < 64
    z = jnp.zeros((64, 128), F32)
    linv0 = jnp.where(left, 0.0, t0)
    uinv0 = jnp.where(left, b0, 0.0)
    u01 = jnp.where(left, 0.0, dot3(linv0, jnp.concatenate([z, top], 0)))
    l10 = dot3(jnp.where(left, bot, 0.0), jnp.concatenate([uinv0, z], 0))
    sch = bot - dot3(l10, jnp.concatenate([u01, z], 0))
    t1, b1 = leaf(sch, 64)
    linv0r = pltpu.roll(linv0, 64, 1)
    zl = dot3(l10, jnp.concatenate([linv0r, z], 0))
    zu = dot3(uinv0, jnp.concatenate([u01, z], 0))
    linv1 = jnp.where(left, t1, 0.0)
    uinv1 = jnp.where(left, 0.0, b1)
    linv10 = dot3(linv1, jnp.concatenate([zl, z], 0))
    uinv01 = dot3(zu, jnp.concatenate([z, uinv1], 0))
    packed = jnp.concatenate([jnp.where(left, t0, u01), jnp.where(left, l10, t1)], 0)
    linv = jnp.concatenate([linv0r, pltpu.roll(linv1, 64, 1) - linv10], 0)
    uinv = jnp.concatenate([uinv0 - uinv01, uinv1], 0)
    return packed, linv, uinv


def blk(i):
    return slice(TB * i, TB * (i + 1))


def later(i):
    return slice(TB * (i + 1), NB)


def strip_update(a_ref, li_ref, ui_ref, n):
    us, ls = [], []
    for i in range(n):
        u = a_ref[blk(i), blk(n)]
        l = a_ref[blk(n), blk(i)]
        for j in range(i):
            u = u - dot3(a_ref[blk(i), blk(j)], us[j])
            l = l - dot3(ls[j], a_ref[blk(j), blk(i)])
        us.append(dot3(li_ref[i], u))
        ls.append(dot3(l, ui_ref[i]))
    schur = a_ref[blk(n), blk(n)]
    for u, l in zip(us, ls):
        schur = schur - dot3(l, u)
    for i in range(n):
        a_ref[blk(i), blk(n)] = us[i]
        a_ref[blk(n), blk(i)] = ls[i]
    a_ref[blk(n), blk(n)] = schur


def solve_u(a_ref, li_ref, q_ref, ub_ref, j):
    u = dot3(li_ref[j], q_ref[blk(j), :])
    ub_ref[blk(j), :] = u.astype(BF)
    if j < 3:
        q_ref[later(j), :] = q_ref[later(j), :] - dot3(a_ref[later(j), blk(j)], u)


def solve_l(a_ref, ui_ref, p_ref, lb_ref, j):
    l = dot3(p_ref[:, blk(j)], ui_ref[j])
    lb_ref[:, blk(j)] = l.astype(BF)
    if j < 3:
        p_ref[:, later(j)] = p_ref[:, later(j)] - dot3(l, a_ref[blk(j), later(j)])


def rcopy(src, dst, ss, rs, dev):
    return pltpu.make_async_remote_copy(src_ref=src, dst_ref=dst, send_sem=ss, recv_sem=rs,
                                        device_id=dev, device_id_type=MESH)


def each(lo, hi, fn):
    def one(s, carry):
        fn(s)
        return carry
    lax.fori_loop(lo, hi, one, 0)


class Moves:
    def __init__(self, prows, pcols, w_ref, c_buf, d_buf, q_buf, p_buf, loc_sem, sems):
        self.prows, self.pcols = prows, pcols
        self.row, self.col = lax.axis_index("prow"), lax.axis_index("pcol")
        self.core = lax.rem(self.col, 2)
        self.w, self.c, self.d, self.q, self.p = w_ref, c_buf, d_buf, q_buf, p_buf
        self.loc = loc_sem
        (self.c_send, self.c_recv, self.cz_send, self.cz_recv,
         self.ds_send, self.ds_recv, self.dz_send, self.dz_recv, self.da_send, self.da_recv,
         self.qs_send, self.qs_recv, self.qa_send, self.qa_recv,
         self.ps_send, self.ps_recv, self.pa_send, self.pa_recv, self.px_send, self.px_recv) = sems
        self.root = jnp.logical_and(self.row == 0, self.col == 0)
        self.passer = self.col == jnp.where(self.row == 0, 1, 0)
        self.pass_hi = jnp.where(self.row == 0, pcols - 1, pcols)
        self.has_q = self.col != 0
        self.has_p = self.row != 0

    def up(self, s):
        return lax.rem(self.row + s, self.prows)

    def along(self, s):
        return lax.rem(self.col + s, self.pcols)

    def same_core(self, s):
        return lax.rem(self.col + 2 * s, self.pcols)

    def ready(self):
        barrier = pltpu.get_barrier_semaphore()

        def tell(dev):
            pl.semaphore_signal(barrier, inc=1, device_id=dev, device_id_type=MESH)
        each(1, self.prows, lambda s: tell({"prow": self.up(s)}))

        @pl.when(self.has_p)
        def _():
            each(1, self.pcols, lambda s: tell({"pcol": self.along(s)}))

        @pl.when(jnp.logical_and(self.row == 0, self.col == 1))
        def _():
            tell({"pcol": 0})

        @pl.when(jnp.logical_and(self.row == 0, self.col > 1))
        def _():
            tell({"pcol": 1})
        zero_row = jnp.where(self.col == 0, 1, jnp.where(self.col == 1, self.pcols - 2, 0))
        pl.semaphore_wait(barrier, self.prows - 1 + jnp.where(self.has_p, self.pcols - 1, zero_row))

    def corner(self, ref, half):
        return ref.at[pl.ds(64 * half, 64), pl.ds(0, TB)]

    def part(self, ref, i, part):
        n = HB // self.prows
        top = pl.ds(pl.multiple_of(i * n, n), n)
        low = pl.multiple_of((i // 2) * n, n)
        side = pl.ds(pl.multiple_of(lax.rem(i, 2) * HB, HB), HB)
        if part == 0:
            return ref.at[top, pl.ds(0, HB)]
        if part in (1, 3):
            return ref.at[top, pl.ds(HB + TB * (part // 2), TB)]
        return ref.at[pl.ds(HB + TB * (part // 2 - 1) + low, n), side]

    def corner_out(self, half, s):
        return rcopy(self.corner(self.w, half), self.corner(self.c, half), self.c_send.at[half, s], self.c_recv.at[half],
                     {"prow": self.up(s)})

    def corner_side(self, half):
        return rcopy(self.corner(self.w, half), self.corner(self.c, half), self.cz_send.at[half, 0], self.cz_recv.at[half],
                     {"pcol": 1})

    def corner_on(self, half, s):
        piece = self.corner(self.c, half)
        return rcopy(piece, piece, self.cz_send.at[half, s], self.cz_recv.at[half], {"pcol": self.along(s)})

    def d_out(self, part, s):
        return rcopy(self.part(self.w, self.up(s), part), self.part(self.d, self.up(s), part),
                     self.ds_send.at[part, s], self.ds_recv.at[part], {"prow": self.up(s)})

    def d_side(self, part):
        return rcopy(self.part(self.w, 0, part), self.part(self.d, 0, part),
                     self.dz_send.at[part, 0], self.dz_recv.at[part], {"pcol": 1})

    def d_on(self, part, s):
        piece = self.part(self.d, self.row, part)
        return rcopy(piece, piece, self.dz_send.at[part, s], self.dz_recv.at[part], {"pcol": self.along(s)})

    def d_share(self, part, s):
        piece = self.part(self.d, self.row, part)
        return rcopy(piece, piece, self.da_send.at[part, s], self.da_recv.at[part, self.row], {"prow": self.up(s)})

    def d_from(self, part, s):
        o = self.up(s)
        piece = self.part(self.d, o, part)
        return rcopy(piece, piece, self.da_send.at[part, s], self.da_recv.at[part, o], {"prow": o})

    def own(self, i):
        if i < 2:
            return pltpu.make_async_copy(self.corner(self.w, i), self.corner(self.c, i), self.loc.at[i])
        if i < 2 + PARTS:
            return pltpu.make_async_copy(self.part(self.w, 0, i - 2), self.part(self.d, 0, i - 2), self.loc.at[i])
        if i == OWN_Q:
            return pltpu.make_async_copy(self.q_piece(self.w, 0), self.q_piece(self.q, 0), self.loc.at[i])
        return pltpu.make_async_copy(self.p_piece(self.w, 0), self.p_piece(self.p, 0), self.loc.at[i])

    def q_piece(self, ref, i):
        n = NB // self.prows
        return ref.at[pl.ds(pl.multiple_of(i * n, n), n), :]

    def q_out(self, s):
        o = self.up(s)
        return rcopy(self.q_piece(self.w, o), self.q_piece(self.q, o), self.qs_send.at[s], self.qs_recv, {"prow": o})

    def q_shares(self, fn):
        first = jnp.where(self.row == 0, self.prows, self.prows - self.row)
        each(1, first, lambda s: fn(self.q_share(s)))
        each(first + 1, self.prows, lambda s: fn(self.q_share(s)))

    def q_share(self, s):
        piece = self.q_piece(self.q, self.row)
        return rcopy(piece, piece, self.qa_send.at[s], self.qa_recv.at[self.row], {"prow": self.up(s)})

    def q_from(self, s):
        o = self.up(s)
        piece = self.q_piece(self.q, o)
        return rcopy(piece, piece, self.qa_send.at[s], self.qa_recv.at[o], {"prow": o})

    def p_piece(self, ref, c):
        n = NB // self.pcols
        at = lax.rem(c, 2) * HB + (c // 2) * n
        return ref.at[pl.ds(pl.multiple_of(at, n), n), :]

    def p_half(self, h):
        return self.p.at[pl.ds(pl.multiple_of(h * HB, HB), HB), :]

    def p_out(self, s):
        o = self.along(s)
        return rcopy(self.p_piece(self.w, o), self.p_piece(self.p, o), self.ps_send.at[s], self.ps_recv, {"pcol": o})

    def p_share(self, s):
        piece = self.p_piece(self.p, self.col)
        return rcopy(piece, piece, self.pa_send.at[s], self.pa_recv.at[self.col // 2], {"pcol": self.same_core(s)})

    def p_from(self, s):
        o = self.same_core(s)
        piece = self.p_piece(self.p, o)
        return rcopy(piece, piece, self.pa_send.at[s], self.pa_recv.at[o // 2], {"pcol": o})

    def p_whole(self):
        return rcopy(self.w, self.p, self.px_send, self.px_recv, {"pcol": 1})

    def p_swap(self):
        mine = self.p_half(self.core)
        return rcopy(mine, mine, self.px_send, self.px_recv, {"pcol": self.col + 1 - 2 * self.core})

    def p_swapped(self):
        other = self.p_half(1 - self.core)
        return rcopy(other, other, self.px_send, self.px_recv, {"pcol": self.col + 1 - 2 * self.core})

    def start(self):
        @pl.when(self.root)
        def _():
            for half in range(2):
                if half == 1:
                    self.root_part(0)
                each(1, self.prows, lambda s: self.corner_out(half, s).start())
                self.corner_side(half).start()
                self.own(half).start()
            for part in range(1, PARTS):
                self.root_part(part)

        @pl.when(jnp.logical_and(self.row == 0, self.col > 1))
        def _():
            self.send_q()

        @pl.when(self.passer)
        def _():
            for half in range(2):
                if half == 1:
                    self.pass_part(0)
                @pl.when(self.has_p)
                def _():
                    self.corner_out(half, 0).wait_recv()

                @pl.when(jnp.logical_not(self.has_p))
                def _():
                    self.corner_side(half).wait_recv()
                each(1, self.pass_hi, lambda s: self.corner_on(half, s).start())

    def root_part(self, part):
        each(1, self.prows, lambda s: self.d_out(part, s).start())
        self.d_side(part).start()
        self.own(2 + part).start()

    def pass_part(self, part):
        @pl.when(self.has_p)
        def _():
            self.d_out(part, 0).wait_recv()

        @pl.when(jnp.logical_not(self.has_p))
        def _():
            self.d_side(part).wait_recv()
        each(1, self.pass_hi, lambda s: self.d_on(part, s).start())

    def pass_rest(self):
        @pl.when(self.passer)
        def _():
            for part in range(1, PARTS):
                self.pass_part(part)

            @pl.when(self.has_p)
            def _():
                each(2, self.pcols, lambda s: self.p_out(s).start())
                self.own(OWN_P).start()
                self.p_whole().start()

            @pl.when(jnp.logical_not(self.has_p))
            def _():
                self.send_q()

    def send_q(self):
        each(1, self.prows, lambda s: self.q_out(s).start())
        self.own(OWN_Q).start()

    def wait_corner(self, half):
        @pl.when(self.root)
        def _():
            self.own(half).wait()

        @pl.when(jnp.logical_not(jnp.logical_or(self.root, self.passer)))
        def _():
            self.corner_on(half, 0).wait_recv()

    def share_d(self, parts):
        for part in parts:
            @pl.when(self.root)
            def _():
                self.own(2 + part).wait()

            @pl.when(jnp.logical_not(jnp.logical_or(self.root, self.passer)))
            def _():
                self.d_on(part, 0).wait_recv()
            each(1, self.prows, lambda s: self.d_share(part, s).start())

    def get_d(self, part):
        each(1, self.prows, lambda s: self.d_from(part, s).wait_recv())

    def share_q(self):
        @pl.when(self.has_q)
        def _():
            @pl.when(self.row == 0)
            def _():
                self.own(OWN_Q).wait()

            @pl.when(self.row != 0)
            def _():
                self.q_out(0).wait_recv()
            self.q_shares(lambda copy: copy.start())

    def get_q(self, q_ref):
        @pl.when(self.row == 0)
        def _():
            q_ref[...] = self.w[...].astype(F32)

        @pl.when(self.row != 0)
        def _():
            each(1, self.prows, lambda s: self.q_from(s).wait_recv())
            q_ref[...] = self.q[...].astype(F32)

    def share_p(self):
        @pl.when(self.has_p)
        def _():
            @pl.when(self.col == 1)
            def _():
                self.p_whole().wait_recv()

            @pl.when(self.col > 1)
            def _():
                self.p_out(0).wait_recv()
            @pl.when(self.col == 0)
            def _():
                self.own(OWN_P).wait()
            self.p_shares(lambda copy: copy.start())

    def p_shares(self, fn):
        chips = self.pcols // 2
        mine = self.col // 2
        each(1, jnp.where(mine == 0, chips, chips - mine), lambda s: fn(self.p_share(s)))
        each(jnp.where(mine == 0, chips, chips - mine + 1), chips, lambda s: fn(self.p_share(s)))

    def swap_p(self):
        @pl.when(self.has_p)
        def _():
            @pl.when(self.col > 1)
            def _():
                each(1, self.pcols // 2, lambda s: self.p_from(s).wait_recv())
                self.p_swap().start()

    def get_p(self, p_ref):
        @pl.when(self.col == 0)
        def _():
            p_ref[...] = self.w[...].astype(F32)

        @pl.when(self.col > 1)
        def _():
            self.p_swapped().wait_recv()

        @pl.when(self.col != 0)
        def _():
            p_ref[...] = self.p[...].astype(F32)

    def finish(self):
        @pl.when(self.root)
        def _():
            for half in range(2):
                each(1, self.prows, lambda s: self.corner_out(half, s).wait_send())
                self.corner_side(half).wait_send()
            for part in range(PARTS):
                each(1, self.prows, lambda s: self.d_out(part, s).wait_send())
                self.d_side(part).wait_send()

        @pl.when(self.passer)
        def _():
            for half in range(2):
                each(1, self.pass_hi, lambda s: self.corner_on(half, s).wait_send())
            for part in range(PARTS):
                each(1, self.pass_hi, lambda s: self.d_on(part, s).wait_send())

            @pl.when(self.has_p)
            def _():
                each(2, self.pcols, lambda s: self.p_out(s).wait_send())
        for part in range(PARTS):
            each(1, self.prows, lambda s: self.d_share(part, s).wait_send())

        @pl.when(self.has_q)
        def _():
            @pl.when(self.row == 0)
            def _():
                each(1, self.prows, lambda s: self.q_out(s).wait_send())
            self.q_shares(lambda copy: copy.wait_send())

        @pl.when(self.has_p)
        def _():
            self.p_shares(lambda copy: copy.wait_send())

            @pl.when(self.col == 0)
            def _():
                self.p_whole().wait_send()

            @pl.when(self.col > 1)
            def _():
                self.p_swap().wait_send()


def step_kernel(prows, pcols, w_hbm, o_ref, w_ref, a_ref, q_ref, p_ref, li_ref, ui_ref, ub_ref, lb_ref,
                c_buf, d_buf, q_buf, p_buf, loc_sem, *sems):
    mv = Moves(prows, pcols, w_ref, c_buf, d_buf, q_buf, p_buf, loc_sem, sems)
    load = pltpu.make_async_copy(w_hbm, w_ref, loc_sem.at[OWN_P + 1])
    load.start()
    mv.ready()
    load.wait()
    mv.start()
    mv.wait_corner(0)
    a_ref[0:64, 0:TB] = c_buf[0:64, :].astype(F32)

    def tile_step(k, carry):
        at = pl.ds(pl.multiple_of(k * TB, TB), TB)
        upper = pl.ds(pl.multiple_of(k * TB, 64), 64)
        lower = pl.ds(pl.multiple_of(k * TB + 64, 64), 64)
        top = a_ref[upper, at]
        t0, b0 = leaf(top, 0)

        @pl.when(k == 0)
        def _():
            mv.share_d([0])
            mv.wait_corner(1)
            a_ref[64:TB, 0:TB] = c_buf[64:TB, :].astype(F32)
            mv.pass_rest()

        @pl.when(k == 1)
        def _():
            mv.share_d([3, 4])
            mv.share_p()

        @pl.when(k == 3)
        def _():
            @pl.when(mv.has_q)
            def _():
                mv.get_q(q_ref)
                for j in range(3):
                    solve_u(a_ref, li_ref, q_ref, ub_ref, j)

            @pl.when(mv.has_p)
            def _():
                mv.get_p(p_ref)
                for j in range(3):
                    solve_l(a_ref, ui_ref, p_ref, lb_ref, j)

        packed, linv, uinv = second_half(t0, b0, top, a_ref[lower, at])
        a_ref[at, at] = packed
        li_ref[k] = linv
        ui_ref[k] = uinv

        @pl.when(k == 0)
        def _():
            mv.share_d([1, 2])
            mv.get_d(0)
            a_ref[0:TB, TB:HB] = d_buf[0:TB, TB:HB].astype(F32)
            a_ref[TB:HB, 0:HB] = d_buf[TB:HB, 0:HB].astype(F32)
            strip_update(a_ref, li_ref, ui_ref, 1)

        @pl.when(k == 1)
        def _():
            mv.share_q()
            mv.get_d(1)
            mv.get_d(2)
            a_ref[0:HB, HB:HB + TB] = d_buf[0:HB, HB:HB + TB].astype(F32)
            a_ref[HB:HB + TB, 0:HB + TB] = d_buf[HB:HB + TB, 0:HB + TB].astype(F32)
            strip_update(a_ref, li_ref, ui_ref, 2)

        @pl.when(k == 2)
        def _():
            mv.swap_p()
            mv.get_d(3)
            mv.get_d(4)
            a_ref[0:HB + TB, HB + TB:NB] = d_buf[0:HB + TB, HB + TB:NB].astype(F32)
            a_ref[HB + TB:NB, :] = d_buf[HB + TB:NB, :].astype(F32)
            strip_update(a_ref, li_ref, ui_ref, 3)
        return carry

    lax.fori_loop(0, 4, tile_step, 0)

    @pl.when(mv.has_q)
    def _():
        solve_u(a_ref, li_ref, q_ref, ub_ref, 3)

    @pl.when(mv.has_p)
    def _():
        solve_l(a_ref, ui_ref, p_ref, lb_ref, 3)

    @pl.when(jnp.logical_and(mv.has_p, mv.has_q))
    def _():
        o_ref[...] = (w_ref[...].astype(F32) - dot(lb_ref[...], ub_ref[...])).astype(BF)

    @pl.when(jnp.logical_and(jnp.logical_not(mv.has_p), mv.has_q))
    def _():
        o_ref[...] = ub_ref[...]

    @pl.when(jnp.logical_and(mv.has_p, jnp.logical_not(mv.has_q)))
    def _():
        o_ref[...] = lb_ref[...]

    @pl.when(mv.root)
    def _():
        o_ref[...] = a_ref[...].astype(BF)

    mv.finish()


def per_device(matrix):
    prows, pcols = lax.axis_size("prow"), lax.axis_size("pcol")
    dma = pltpu.SemaphoreType.DMA
    out = pl.pallas_call(
        functools.partial(step_kernel, prows, pcols),
        out_shape=pltpu.VMEM((NB, NB), BF),
        in_specs=[pl.BlockSpec(memory_space=pl.ANY)],
        out_specs=pl.BlockSpec(memory_space=pltpu.VMEM),
        scratch_shapes=[
            pltpu.VMEM((NB, NB), BF),
            pltpu.VMEM((NB, NB), F32), pltpu.VMEM((NB, NB), F32), pltpu.VMEM((NB, NB), F32),
            pltpu.VMEM((4, TB, TB), F32), pltpu.VMEM((4, TB, TB), F32),
            pltpu.VMEM((NB, NB), BF), pltpu.VMEM((NB, NB), BF),
            pltpu.VMEM((TB, TB), BF), pltpu.VMEM((NB, NB), BF), pltpu.VMEM((NB, NB), BF), pltpu.VMEM((NB, NB), BF),
            dma((5 + PARTS,)),
            dma((2, prows)), dma((2,)), dma((2, pcols)), dma((2,)),
            dma((PARTS, prows)), dma((PARTS,)), dma((PARTS, pcols)), dma((PARTS,)), dma((PARTS, prows)), dma((PARTS, prows)),
            dma((prows,)), dma, dma((prows,)), dma((prows,)),
            dma((pcols,)), dma, dma((pcols // 2,)), dma((pcols // 2,)), dma, dma,
        ],
        compiler_params=pltpu.CompilerParams(collective_id=0, has_side_effects=True),
    )(matrix.reshape(NB, NB))
    return out.reshape(matrix.shape)


def solution(mesh):
    placed = P(None, "prow", None, "pcol")
    return jax.shard_map(per_device, mesh=mesh, in_specs=(placed,), out_specs=placed, check_vma=False)
```

```python
import functools

import jax
import jax.numpy as jnp
from jax import lax
from jax.experimental import pallas as pl
from jax.experimental.pallas import tpu as pltpu
from jax.sharding import PartitionSpec as P

F32 = jnp.float32
BF = jnp.bfloat16
NB = 512
HB = 256
TB = 128
PARTS = 5
OWN_Q, OWN_P = 2 + PARTS, 3 + PARTS
MESH = pl.DeviceIdType.MESH


def split(x):
    hi = x.astype(BF)
    lo = (x - hi.astype(F32)).astype(BF)
    return hi, lo

def dot(a, b):
    return jnp.dot(a, b, preferred_element_type=F32)

def dot3s(a, b):
    ah, al = a; bh, bl = b
    return dot(jnp.concatenate([ah, al, ah], 1), jnp.concatenate([bh, bh, bl], 0))

def dot3(a, b):
    return dot3s(split(a), split(b))

def iotas(rows=8):
    return (lax.broadcasted_iota(jnp.int32, (rows, 128), 0), lax.broadcasted_iota(jnp.int32, (rows, 128), 1))

def leaf(block, base):
    sub, lane = iotas()
    other = 64 - base
    tiles = []
    for t in range(8):
        eye = jnp.where(lane == other + 8 * t + sub, 1.0, 0.0)
        keep = (lane >= base) & (lane < base + 64)
        tiles.append(jnp.where(keep, block[8 * t:8 * t + 8, :], eye))
    low = [None] * 8
    for g in range(8):
        c0 = base + 8 * g
        inside = (lane >= c0) & (lane < c0 + 8)
        grp = tiles[g]
        cols = [jnp.broadcast_to(grp[:, c0 + j:c0 + j + 1], (8, 128)) for j in range(8)]
        outer = {}
        for t in list(range(g + 1, 8)) + [8 + s for s in range(g)]:
            src = tiles[t] if t < 8 else low[t - 8]
            outer[t] = [jnp.broadcast_to(src[:, c0 + j:c0 + j + 1], (8, 128)) for j in range(8)]
        done = (lane >= base) & (lane < c0)
        held = grp
        grp = jnp.where(done, 0.0, grp)
        mult = jnp.zeros((8, 128), F32)
        v = jnp.where(inside, jnp.where(lane == c0 + sub, 1.0, 0.0), grp)
        scale = jnp.zeros((8, 128), F32)
        for j in range(8):
            piv = jnp.broadcast_to(cols[j][j:j + 1, :], (8, 128))
            rcp = 1.0 / piv
            m = jnp.where(sub == j, 0.0, cols[j] * rcp)
            for i in range(j + 1, 8):
                cols[i] = cols[i] - m * jnp.broadcast_to(cols[i][j:j + 1, :], (8, 128))
            mlow = jnp.where(sub > j, m, 0.0)
            grp = grp - mlow * jnp.broadcast_to(grp[j:j + 1, :], (8, 128))
            mult = jnp.where(lane == c0 + j, m, mult)
            mv = jnp.where(inside & (sub > j), 0.0, m)
            v = v - mv * jnp.broadcast_to(v[j:j + 1, :], (8, 128))
            scale = jnp.where(sub == j, rcp, scale)
        grp = jnp.where(inside & (lane < c0 + sub), mult, grp)
        tiles[g] = jnp.where(done, held, grp)
        v = v * scale
        v = jnp.where(inside, -v, v)
        rows = [jnp.broadcast_to(v[j:j + 1, :], (8, 128)) for j in range(8)]
        for t, cs in outer.items():
            src = tiles[t] if t < 8 else low[t - 8]
            p = [cs[j] * rows[j] for j in range(8)]
            tot = ((p[0] + p[1]) + (p[2] + p[3])) + ((p[4] + p[5]) + (p[6] + p[7]))
            new = jnp.where(inside, 0.0, src) - tot
            if t < 8:
                tiles[t] = new
            else:
                low[t - 8] = new
        low[g] = -v
    return jnp.concatenate(tiles, 0), jnp.concatenate(low, 0)


def second_half(t0, b0, top, bot):
    _, lane = iotas(64)
    left = lane < 64
    z = jnp.zeros((64, 128), F32)
    linv0 = jnp.where(left, 0.0, t0)
    uinv0 = jnp.where(left, b0, 0.0)
    u01 = jnp.where(left, 0.0, dot3(linv0, jnp.concatenate([z, top], 0)))
    l10 = dot3(jnp.where(left, bot, 0.0), jnp.concatenate([uinv0, z], 0))
    sch = bot - dot3(l10, jnp.concatenate([u01, z], 0))
    t1, b1 = leaf(sch, 64)
    linv0r = pltpu.roll(linv0, 64, 1)
    zl = dot3(l10, jnp.concatenate([linv0r, z], 0))
    zu = dot3(uinv0, jnp.concatenate([u01, z], 0))
    linv1 = jnp.where(left, t1, 0.0)
    uinv1 = jnp.where(left, 0.0, b1)
    linv10 = dot3(linv1, jnp.concatenate([zl, z], 0))
    uinv01 = dot3(zu, jnp.concatenate([z, uinv1], 0))
    packed = jnp.concatenate([jnp.where(left, t0, u01), jnp.where(left, l10, t1)], 0)
    linv = jnp.concatenate([linv0r, pltpu.roll(linv1, 64, 1) - linv10], 0)
    uinv = jnp.concatenate([uinv0 - uinv01, uinv1], 0)
    return packed, linv, uinv


def blk(i):
    return slice(TB * i, TB * (i + 1))


def later(i):
    return slice(TB * (i + 1), NB)


def strip_update(a_ref, li_ref, ui_ref, n):
    us, ls = [], []
    for i in range(n):
        u = a_ref[blk(i), blk(n)]
        l = a_ref[blk(n), blk(i)]
        for j in range(i):
            u = u - dot3(a_ref[blk(i), blk(j)], us[j])
            l = l - dot3(ls[j], a_ref[blk(j), blk(i)])
        us.append(dot3(li_ref[i], u))
        ls.append(dot3(l, ui_ref[i]))
    schur = a_ref[blk(n), blk(n)]
    for u, l in zip(us, ls):
        schur = schur - dot3(l, u)
    for i in range(n):
        a_ref[blk(i), blk(n)] = us[i]
        a_ref[blk(n), blk(i)] = ls[i]
    a_ref[blk(n), blk(n)] = schur


def solve_u(a_ref, li_ref, q_ref, ub_ref, j):
    u = dot3(li_ref[j], q_ref[blk(j), :])
    ub_ref[blk(j), :] = u.astype(BF)
    if j < 3:
        q_ref[later(j), :] = q_ref[later(j), :] - dot3(a_ref[later(j), blk(j)], u)


def solve_l(a_ref, ui_ref, p_ref, lb_ref, j):
    l = dot3(p_ref[:, blk(j)], ui_ref[j])
    lb_ref[:, blk(j)] = l.astype(BF)
    if j < 3:
        p_ref[:, later(j)] = p_ref[:, later(j)] - dot3(l, a_ref[blk(j), later(j)])


def rcopy(src, dst, ss, rs, dev):
    return pltpu.make_async_remote_copy(src_ref=src, dst_ref=dst, send_sem=ss, recv_sem=rs,
                                        device_id=dev, device_id_type=MESH)


def each(lo, hi, fn):
    def one(s, carry):
        fn(s)
        return carry
    lax.fori_loop(lo, hi, one, 0)


class Moves:
    def __init__(self, prows, pcols, w_ref, c_buf, d_buf, q_buf, p_buf, loc_sem, sems):
        self.prows, self.pcols = prows, pcols
        self.row, self.col = lax.axis_index("prow"), lax.axis_index("pcol")
        self.core = lax.rem(self.col, 2)
        self.w, self.c, self.d, self.q, self.p = w_ref, c_buf, d_buf, q_buf, p_buf
        self.loc = loc_sem
        (self.c_send, self.c_recv, self.cz_send, self.cz_recv,
         self.ds_send, self.ds_recv, self.dz_send, self.dz_recv, self.da_send, self.da_recv,
         self.qs_send, self.qs_recv, self.qa_send, self.qa_recv,
         self.ps_send, self.ps_recv, self.pa_send, self.pa_recv, self.px_send, self.px_recv) = sems
        self.root = jnp.logical_and(self.row == 0, self.col == 0)
        self.passer = self.col == jnp.where(self.row == 0, 1, 0)
        self.pass_hi = jnp.where(self.row == 0, pcols - 1, pcols)
        self.has_q = self.col != 0
        self.has_p = self.row != 0

    def up(self, s):
        return lax.rem(self.row + s, self.prows)

    def along(self, s):
        return lax.rem(self.col + s, self.pcols)

    def same_core(self, s):
        return lax.rem(self.col + 2 * s, self.pcols)

    def ready(self):
        barrier = pltpu.get_barrier_semaphore()

        def tell(dev):
            pl.semaphore_signal(barrier, inc=1, device_id=dev, device_id_type=MESH)
        each(1, self.prows, lambda s: tell({"prow": self.up(s)}))

        @pl.when(self.has_p)
        def _():
            each(1, self.pcols, lambda s: tell({"pcol": self.along(s)}))

        @pl.when(jnp.logical_and(self.row == 0, self.col == 1))
        def _():
            tell({"pcol": 0})

        @pl.when(jnp.logical_and(self.row == 0, self.col > 1))
        def _():
            tell({"pcol": 1})
        zero_row = jnp.where(self.col == 0, 1, jnp.where(self.col == 1, self.pcols - 2, 0))
        pl.semaphore_wait(barrier, self.prows - 1 + jnp.where(self.has_p, self.pcols - 1, zero_row))

    def corner(self, ref, half):
        return ref.at[pl.ds(64 * half, 64), pl.ds(0, TB)]

    def part(self, ref, i, part):
        n = HB // self.prows
        top = pl.ds(pl.multiple_of(i * n, n), n)
        low = pl.multiple_of((i // 2) * n, n)
        side = pl.ds(pl.multiple_of(lax.rem(i, 2) * HB, HB), HB)
        if part == 0:
            return ref.at[top, pl.ds(0, HB)]
        if part in (1, 3):
            return ref.at[top, pl.ds(HB + TB * (part // 2), TB)]
        return ref.at[pl.ds(HB + TB * (part // 2 - 1) + low, n), side]

    def corner_out(self, half, s):
        return rcopy(self.corner(self.w, half), self.corner(self.c, half), self.c_send.at[half, s], self.c_recv.at[half],
                     {"prow": self.up(s)})

    def corner_side(self, half):
        return rcopy(self.corner(self.w, half), self.corner(self.c, half), self.cz_send.at[half, 0], self.cz_recv.at[half],
                     {"pcol": 1})

    def corner_on(self, half, s):
        piece = self.corner(self.c, half)
        return rcopy(piece, piece, self.cz_send.at[half, s], self.cz_recv.at[half], {"pcol": self.along(s)})

    def d_out(self, part, s):
        return rcopy(self.part(self.w, self.up(s), part), self.part(self.d, self.up(s), part),
                     self.ds_send.at[part, s], self.ds_recv.at[part], {"prow": self.up(s)})

    def d_side(self, part):
        return rcopy(self.part(self.w, 0, part), self.part(self.d, 0, part),
                     self.dz_send.at[part, 0], self.dz_recv.at[part], {"pcol": 1})

    def d_on(self, part, s):
        piece = self.part(self.d, self.row, part)
        return rcopy(piece, piece, self.dz_send.at[part, s], self.dz_recv.at[part], {"pcol": self.along(s)})

    def d_share(self, part, s):
        piece = self.part(self.d, self.row, part)
        return rcopy(piece, piece, self.da_send.at[part, s], self.da_recv.at[part, self.row], {"prow": self.up(s)})

    def d_from(self, part, s):
        o = self.up(s)
        piece = self.part(self.d, o, part)
        return rcopy(piece, piece, self.da_send.at[part, s], self.da_recv.at[part, o], {"prow": o})

    def own(self, i):
        if i < 2:
            return pltpu.make_async_copy(self.corner(self.w, i), self.corner(self.c, i), self.loc.at[i])
        if i < 2 + PARTS:
            return pltpu.make_async_copy(self.part(self.w, 0, i - 2), self.part(self.d, 0, i - 2), self.loc.at[i])
        if i == OWN_Q:
            return pltpu.make_async_copy(self.q_piece(self.w, 0), self.q_piece(self.q, 0), self.loc.at[i])
        return pltpu.make_async_copy(self.p_piece(self.w, 0), self.p_piece(self.p, 0), self.loc.at[i])

    def q_piece(self, ref, i):
        n = NB // self.prows
        return ref.at[pl.ds(pl.multiple_of(i * n, n), n), :]

    def q_out(self, s):
        o = self.up(s)
        return rcopy(self.q_piece(self.w, o), self.q_piece(self.q, o), self.qs_send.at[s], self.qs_recv, {"prow": o})

    def q_shares(self, fn):
        first = jnp.where(self.row == 0, self.prows, self.prows - self.row)
        each(1, first, lambda s: fn(self.q_share(s)))
        each(first + 1, self.prows, lambda s: fn(self.q_share(s)))

    def q_share(self, s):
        piece = self.q_piece(self.q, self.row)
        return rcopy(piece, piece, self.qa_send.at[s], self.qa_recv.at[self.row], {"prow": self.up(s)})

    def q_from(self, s):
        o = self.up(s)
        piece = self.q_piece(self.q, o)
        return rcopy(piece, piece, self.qa_send.at[s], self.qa_recv.at[o], {"prow": o})

    def p_piece(self, ref, c):
        n = NB // self.pcols
        at = lax.rem(c, 2) * HB + (c // 2) * n
        return ref.at[pl.ds(pl.multiple_of(at, n), n), :]

    def p_half(self, h):
        return self.p.at[pl.ds(pl.multiple_of(h * HB, HB), HB), :]

    def p_out(self, s):
        o = self.along(s)
        return rcopy(self.p_piece(self.w, o), self.p_piece(self.p, o), self.ps_send.at[s], self.ps_recv, {"pcol": o})

    def p_share(self, s):
        piece = self.p_piece(self.p, self.col)
        return rcopy(piece, piece, self.pa_send.at[s], self.pa_recv.at[self.col // 2], {"pcol": self.same_core(s)})

    def p_from(self, s):
        o = self.same_core(s)
        piece = self.p_piece(self.p, o)
        return rcopy(piece, piece, self.pa_send.at[s], self.pa_recv.at[o // 2], {"pcol": o})

    def p_whole(self):
        return rcopy(self.w, self.p, self.px_send, self.px_recv, {"pcol": 1})

    def p_swap(self):
        mine = self.p_half(self.core)
        return rcopy(mine, mine, self.px_send, self.px_recv, {"pcol": self.col + 1 - 2 * self.core})

    def p_swapped(self):
        other = self.p_half(1 - self.core)
        return rcopy(other, other, self.px_send, self.px_recv, {"pcol": self.col + 1 - 2 * self.core})

    def start(self):
        @pl.when(self.root)
        def _():
            self.root_part(0)
            for half in range(2):
                each(1, self.prows, lambda s: self.corner_out(half, s).start())
                self.corner_side(half).start()
                self.own(half).start()
            for part in range(1, PARTS):
                self.root_part(part)

        @pl.when(jnp.logical_and(self.row == 0, self.col > 1))
        def _():
            self.send_q()

        @pl.when(self.passer)
        def _():
            self.pass_part(0)
            for half in range(2):
                @pl.when(self.has_p)
                def _():
                    self.corner_out(half, 0).wait_recv()

                @pl.when(jnp.logical_not(self.has_p))
                def _():
                    self.corner_side(half).wait_recv()
                each(1, self.pass_hi, lambda s: self.corner_on(half, s).start())

    def root_part(self, part):
        each(1, self.prows, lambda s: self.d_out(part, s).start())
        self.d_side(part).start()
        self.own(2 + part).start()

    def pass_part(self, part):
        @pl.when(self.has_p)
        def _():
            self.d_out(part, 0).wait_recv()

        @pl.when(jnp.logical_not(self.has_p))
        def _():
            self.d_side(part).wait_recv()
        each(1, self.pass_hi, lambda s: self.d_on(part, s).start())

    def pass_rest(self):
        @pl.when(self.passer)
        def _():
            for part in range(1, PARTS):
                self.pass_part(part)

            @pl.when(self.has_p)
            def _():
                each(2, self.pcols, lambda s: self.p_out(s).start())
                self.own(OWN_P).start()
                self.p_whole().start()

            @pl.when(jnp.logical_not(self.has_p))
            def _():
                self.send_q()

    def send_q(self):
        each(1, self.prows, lambda s: self.q_out(s).start())
        self.own(OWN_Q).start()

    def wait_corner(self, half):
        @pl.when(self.root)
        def _():
            self.own(half).wait()

        @pl.when(jnp.logical_not(jnp.logical_or(self.root, self.passer)))
        def _():
            self.corner_on(half, 0).wait_recv()

    def share_d(self, parts):
        for part in parts:
            @pl.when(self.root)
            def _():
                self.own(2 + part).wait()

            @pl.when(jnp.logical_not(jnp.logical_or(self.root, self.passer)))
            def _():
                self.d_on(part, 0).wait_recv()
            each(1, self.prows, lambda s: self.d_share(part, s).start())

    def get_d(self, part):
        each(1, self.prows, lambda s: self.d_from(part, s).wait_recv())

    def share_q(self):
        @pl.when(self.has_q)
        def _():
            @pl.when(self.row == 0)
            def _():
                self.own(OWN_Q).wait()

            @pl.when(self.row != 0)
            def _():
                self.q_out(0).wait_recv()
            self.q_shares(lambda copy: copy.start())

    def get_q(self, q_ref):
        @pl.when(self.row == 0)
        def _():
            q_ref[...] = self.w[...].astype(F32)

        @pl.when(self.row != 0)
        def _():
            each(1, self.prows, lambda s: self.q_from(s).wait_recv())
            q_ref[...] = self.q[...].astype(F32)

    def share_p(self):
        @pl.when(self.has_p)
        def _():
            @pl.when(self.col == 1)
            def _():
                self.p_whole().wait_recv()

            @pl.when(self.col > 1)
            def _():
                self.p_out(0).wait_recv()
            @pl.when(self.col == 0)
            def _():
                self.own(OWN_P).wait()
            self.p_shares(lambda copy: copy.start())

    def p_shares(self, fn):
        chips = self.pcols // 2
        mine = self.col // 2
        each(1, jnp.where(mine == 0, chips, chips - mine), lambda s: fn(self.p_share(s)))
        each(jnp.where(mine == 0, chips, chips - mine + 1), chips, lambda s: fn(self.p_share(s)))

    def swap_p(self):
        @pl.when(self.has_p)
        def _():
            @pl.when(self.col > 1)
            def _():
                each(1, self.pcols // 2, lambda s: self.p_from(s).wait_recv())
                self.p_swap().start()

    def get_p(self, p_ref):
        @pl.when(self.col == 0)
        def _():
            p_ref[...] = self.w[...].astype(F32)

        @pl.when(self.col > 1)
        def _():
            self.p_swapped().wait_recv()

        @pl.when(self.col != 0)
        def _():
            p_ref[...] = self.p[...].astype(F32)

    def finish(self):
        @pl.when(self.root)
        def _():
            for half in range(2):
                each(1, self.prows, lambda s: self.corner_out(half, s).wait_send())
                self.corner_side(half).wait_send()
            for part in range(PARTS):
                each(1, self.prows, lambda s: self.d_out(part, s).wait_send())
                self.d_side(part).wait_send()

        @pl.when(self.passer)
        def _():
            for half in range(2):
                each(1, self.pass_hi, lambda s: self.corner_on(half, s).wait_send())
            for part in range(PARTS):
                each(1, self.pass_hi, lambda s: self.d_on(part, s).wait_send())

            @pl.when(self.has_p)
            def _():
                each(2, self.pcols, lambda s: self.p_out(s).wait_send())
        for part in range(PARTS):
            each(1, self.prows, lambda s: self.d_share(part, s).wait_send())

        @pl.when(self.has_q)
        def _():
            @pl.when(self.row == 0)
            def _():
                each(1, self.prows, lambda s: self.q_out(s).wait_send())
            self.q_shares(lambda copy: copy.wait_send())

        @pl.when(self.has_p)
        def _():
            self.p_shares(lambda copy: copy.wait_send())

            @pl.when(self.col == 0)
            def _():
                self.p_whole().wait_send()

            @pl.when(self.col > 1)
            def _():
                self.p_swap().wait_send()


def step_kernel(prows, pcols, w_hbm, o_ref, w_ref, a_ref, q_ref, p_ref, li_ref, ui_ref, ub_ref, lb_ref,
                c_buf, d_buf, q_buf, p_buf, loc_sem, *sems):
    mv = Moves(prows, pcols, w_ref, c_buf, d_buf, q_buf, p_buf, loc_sem, sems)
    load = pltpu.make_async_copy(w_hbm, w_ref, loc_sem.at[OWN_P + 1])
    load.start()
    mv.ready()
    load.wait()
    mv.start()
    mv.share_d([0])
    mv.wait_corner(0)
    a_ref[0:64, 0:TB] = c_buf[0:64, :].astype(F32)

    def tile_step(k, carry):
        at = pl.ds(pl.multiple_of(k * TB, TB), TB)
        upper = pl.ds(pl.multiple_of(k * TB, 64), 64)
        lower = pl.ds(pl.multiple_of(k * TB + 64, 64), 64)
        top = a_ref[upper, at]
        t0, b0 = leaf(top, 0)

        @pl.when(k == 0)
        def _():
            mv.wait_corner(1)
            a_ref[64:TB, 0:TB] = c_buf[64:TB, :].astype(F32)
            mv.pass_rest()

        @pl.when(k == 1)
        def _():
            mv.share_d([3, 4])
            mv.share_p()

        @pl.when(k == 3)
        def _():
            @pl.when(mv.has_q)
            def _():
                mv.get_q(q_ref)
                for j in range(3):
                    solve_u(a_ref, li_ref, q_ref, ub_ref, j)

            @pl.when(mv.has_p)
            def _():
                mv.get_p(p_ref)
                for j in range(3):
                    solve_l(a_ref, ui_ref, p_ref, lb_ref, j)

        packed, linv, uinv = second_half(t0, b0, top, a_ref[lower, at])
        a_ref[at, at] = packed
        li_ref[k] = linv
        ui_ref[k] = uinv

        @pl.when(k == 0)
        def _():
            mv.share_d([1, 2])
            mv.get_d(0)
            a_ref[0:TB, TB:HB] = d_buf[0:TB, TB:HB].astype(F32)
            a_ref[TB:HB, 0:HB] = d_buf[TB:HB, 0:HB].astype(F32)
            strip_update(a_ref, li_ref, ui_ref, 1)

        @pl.when(k == 1)
        def _():
            mv.share_q()
            mv.get_d(1)
            mv.get_d(2)
            a_ref[0:HB, HB:HB + TB] = d_buf[0:HB, HB:HB + TB].astype(F32)
            a_ref[HB:HB + TB, 0:HB + TB] = d_buf[HB:HB + TB, 0:HB + TB].astype(F32)
            strip_update(a_ref, li_ref, ui_ref, 2)

        @pl.when(k == 2)
        def _():
            mv.get_d(3)
            mv.get_d(4)
            mv.swap_p()
            a_ref[0:HB + TB, HB + TB:NB] = d_buf[0:HB + TB, HB + TB:NB].astype(F32)
            a_ref[HB + TB:NB, :] = d_buf[HB + TB:NB, :].astype(F32)
            strip_update(a_ref, li_ref, ui_ref, 3)
        return carry

    lax.fori_loop(0, 4, tile_step, 0)

    @pl.when(mv.has_q)
    def _():
        solve_u(a_ref, li_ref, q_ref, ub_ref, 3)

    @pl.when(mv.has_p)
    def _():
        solve_l(a_ref, ui_ref, p_ref, lb_ref, 3)

    @pl.when(jnp.logical_and(mv.has_p, mv.has_q))
    def _():
        o_ref[...] = (w_ref[...].astype(F32) - dot(lb_ref[...], ub_ref[...])).astype(BF)

    @pl.when(jnp.logical_and(jnp.logical_not(mv.has_p), mv.has_q))
    def _():
        o_ref[...] = ub_ref[...]

    @pl.when(jnp.logical_and(mv.has_p, jnp.logical_not(mv.has_q)))
    def _():
        o_ref[...] = lb_ref[...]

    @pl.when(mv.root)
    def _():
        o_ref[...] = a_ref[...].astype(BF)

    mv.finish()


def per_device(matrix):
    prows, pcols = lax.axis_size("prow"), lax.axis_size("pcol")
    dma = pltpu.SemaphoreType.DMA
    out = pl.pallas_call(
        functools.partial(step_kernel, prows, pcols),
        out_shape=pltpu.VMEM((NB, NB), BF),
        in_specs=[pl.BlockSpec(memory_space=pl.ANY)],
        out_specs=pl.BlockSpec(memory_space=pltpu.VMEM),
        scratch_shapes=[
            pltpu.VMEM((NB, NB), BF),
            pltpu.VMEM((NB, NB), F32), pltpu.VMEM((NB, NB), F32), pltpu.VMEM((NB, NB), F32),
            pltpu.VMEM((4, TB, TB), F32), pltpu.VMEM((4, TB, TB), F32),
            pltpu.VMEM((NB, NB), BF), pltpu.VMEM((NB, NB), BF),
            pltpu.VMEM((TB, TB), BF), pltpu.VMEM((NB, NB), BF), pltpu.VMEM((NB, NB), BF), pltpu.VMEM((NB, NB), BF),
            dma((5 + PARTS,)),
            dma((2, prows)), dma((2,)), dma((2, pcols)), dma((2,)),
            dma((PARTS, prows)), dma((PARTS,)), dma((PARTS, pcols)), dma((PARTS,)), dma((PARTS, prows)), dma((PARTS, prows)),
            dma((prows,)), dma, dma((prows,)), dma((prows,)),
            dma((pcols,)), dma, dma((pcols // 2,)), dma((pcols // 2,)), dma, dma,
        ],
        compiler_params=pltpu.CompilerParams(collective_id=0, has_side_effects=True),
    )(matrix.reshape(NB, NB))
    return out.reshape(matrix.shape)


def solution(mesh):
    placed = P(None, "prow", None, "pcol")
    return jax.shard_map(per_device, mesh=mesh, in_specs=(placed,), out_specs=placed, check_vma=False)
```

```python
import functools

import jax
import jax.numpy as jnp
from jax import lax
from jax.experimental import pallas as pl
from jax.experimental.pallas import tpu as pltpu
from jax.sharding import PartitionSpec as P

F32 = jnp.float32
BF = jnp.bfloat16
NB = 512
HB = 256
TB = 128
PARTS = 5
OWN_Q, OWN_P = 2 + PARTS, 3 + PARTS
MESH = pl.DeviceIdType.MESH


def split(x):
    hi = x.astype(BF)
    lo = (x - hi.astype(F32)).astype(BF)
    return hi, lo

def dot(a, b):
    return jnp.dot(a, b, preferred_element_type=F32)

def dot3s(a, b):
    ah, al = a; bh, bl = b
    return dot(jnp.concatenate([ah, al, ah], 1), jnp.concatenate([bh, bh, bl], 0))

def dot3(a, b):
    return dot3s(split(a), split(b))

def iotas(rows=8):
    return (lax.broadcasted_iota(jnp.int32, (rows, 128), 0), lax.broadcasted_iota(jnp.int32, (rows, 128), 1))

def leaf(block, base):
    sub, lane = iotas()
    other = 64 - base
    tiles = []
    for t in range(8):
        eye = jnp.where(lane == other + 8 * t + sub, 1.0, 0.0)
        keep = (lane >= base) & (lane < base + 64)
        tiles.append(jnp.where(keep, block[8 * t:8 * t + 8, :], eye))
    low = [None] * 8
    for g in range(8):
        c0 = base + 8 * g
        inside = (lane >= c0) & (lane < c0 + 8)
        grp = tiles[g]
        cols = [jnp.broadcast_to(grp[:, c0 + j:c0 + j + 1], (8, 128)) for j in range(8)]
        outer = {}
        for t in list(range(g + 1, 8)) + [8 + s for s in range(g)]:
            src = tiles[t] if t < 8 else low[t - 8]
            outer[t] = [jnp.broadcast_to(src[:, c0 + j:c0 + j + 1], (8, 128)) for j in range(8)]
        done = (lane >= base) & (lane < c0)
        held = grp
        grp = jnp.where(done, 0.0, grp)
        mult = jnp.zeros((8, 128), F32)
        v = jnp.where(inside, jnp.where(lane == c0 + sub, 1.0, 0.0), grp)
        scale = jnp.zeros((8, 128), F32)
        for j in range(8):
            piv = jnp.broadcast_to(cols[j][j:j + 1, :], (8, 128))
            rcp = 1.0 / piv
            m = jnp.where(sub == j, 0.0, cols[j] * rcp)
            for i in range(j + 1, 8):
                cols[i] = cols[i] - m * jnp.broadcast_to(cols[i][j:j + 1, :], (8, 128))
            mlow = jnp.where(sub > j, m, 0.0)
            grp = grp - mlow * jnp.broadcast_to(grp[j:j + 1, :], (8, 128))
            mult = jnp.where(lane == c0 + j, m, mult)
            mv = jnp.where(inside & (sub > j), 0.0, m)
            v = v - mv * jnp.broadcast_to(v[j:j + 1, :], (8, 128))
            scale = jnp.where(sub == j, rcp, scale)
        grp = jnp.where(inside & (lane < c0 + sub), mult, grp)
        tiles[g] = jnp.where(done, held, grp)
        v = v * scale
        v = jnp.where(inside, -v, v)
        rows = [jnp.broadcast_to(v[j:j + 1, :], (8, 128)) for j in range(8)]
        for t, cs in outer.items():
            src = tiles[t] if t < 8 else low[t - 8]
            p = [cs[j] * rows[j] for j in range(8)]
            tot = ((p[0] + p[1]) + (p[2] + p[3])) + ((p[4] + p[5]) + (p[6] + p[7]))
            new = jnp.where(inside, 0.0, src) - tot
            if t < 8:
                tiles[t] = new
            else:
                low[t - 8] = new
        low[g] = -v
    return jnp.concatenate(tiles, 0), jnp.concatenate(low, 0)


def second_half(t0, b0, top, bot):
    _, lane = iotas(64)
    left = lane < 64
    z = jnp.zeros((64, 128), F32)
    linv0 = jnp.where(left, 0.0, t0)
    uinv0 = jnp.where(left, b0, 0.0)
    u01 = jnp.where(left, 0.0, dot3(linv0, jnp.concatenate([z, top], 0)))
    l10 = dot3(jnp.where(left, bot, 0.0), jnp.concatenate([uinv0, z], 0))
    sch = bot - dot3(l10, jnp.concatenate([u01, z], 0))
    t1, b1 = leaf(sch, 64)
    linv0r = pltpu.roll(linv0, 64, 1)
    zl = dot3(l10, jnp.concatenate([linv0r, z], 0))
    zu = dot3(uinv0, jnp.concatenate([u01, z], 0))
    linv1 = jnp.where(left, t1, 0.0)
    uinv1 = jnp.where(left, 0.0, b1)
    linv10 = dot3(linv1, jnp.concatenate([zl, z], 0))
    uinv01 = dot3(zu, jnp.concatenate([z, uinv1], 0))
    packed = jnp.concatenate([jnp.where(left, t0, u01), jnp.where(left, l10, t1)], 0)
    linv = jnp.concatenate([linv0r, pltpu.roll(linv1, 64, 1) - linv10], 0)
    uinv = jnp.concatenate([uinv0 - uinv01, uinv1], 0)
    return packed, linv, uinv


def blk(i):
    return slice(TB * i, TB * (i + 1))


def later(i):
    return slice(TB * (i + 1), NB)


def strip_update(a_ref, li_ref, ui_ref, n):
    us, ls = [], []
    for i in range(n):
        u = a_ref[blk(i), blk(n)]
        l = a_ref[blk(n), blk(i)]
        for j in range(i):
            u = u - dot3(a_ref[blk(i), blk(j)], us[j])
            l = l - dot3(ls[j], a_ref[blk(j), blk(i)])
        us.append(dot3(li_ref[i], u))
        ls.append(dot3(l, ui_ref[i]))
    schur = a_ref[blk(n), blk(n)]
    for u, l in zip(us, ls):
        schur = schur - dot3(l, u)
    for i in range(n):
        a_ref[blk(i), blk(n)] = us[i]
        a_ref[blk(n), blk(i)] = ls[i]
    a_ref[blk(n), blk(n)] = schur


def solve_u(a_ref, li_ref, q_ref, ub_ref, j):
    u = dot3(li_ref[j], q_ref[blk(j), :])
    ub_ref[blk(j), :] = u.astype(BF)
    if j < 3:
        q_ref[later(j), :] = q_ref[later(j), :] - dot3(a_ref[later(j), blk(j)], u)


def solve_l(a_ref, ui_ref, p_ref, lb_ref, j):
    l = dot3(p_ref[:, blk(j)], ui_ref[j])
    lb_ref[:, blk(j)] = l.astype(BF)
    if j < 3:
        p_ref[:, later(j)] = p_ref[:, later(j)] - dot3(l, a_ref[blk(j), later(j)])


def rcopy(src, dst, ss, rs, dev):
    return pltpu.make_async_remote_copy(src_ref=src, dst_ref=dst, send_sem=ss, recv_sem=rs,
                                        device_id=dev, device_id_type=MESH)


def each(lo, hi, fn):
    def one(s, carry):
        fn(s)
        return carry
    lax.fori_loop(lo, hi, one, 0)


class Moves:
    def __init__(self, prows, pcols, w_ref, c_buf, d_buf, q_buf, p_buf, loc_sem, sems):
        self.prows, self.pcols = prows, pcols
        self.row, self.col = lax.axis_index("prow"), lax.axis_index("pcol")
        self.core = lax.rem(self.col, 2)
        self.w, self.c, self.d, self.q, self.p = w_ref, c_buf, d_buf, q_buf, p_buf
        self.loc = loc_sem
        (self.c_send, self.c_recv, self.cz_send, self.cz_recv,
         self.ds_send, self.ds_recv, self.dz_send, self.dz_recv, self.da_send, self.da_recv,
         self.qs_send, self.qs_recv, self.qa_send, self.qa_recv,
         self.ps_send, self.ps_recv, self.pa_send, self.pa_recv, self.px_send, self.px_recv) = sems
        self.root = jnp.logical_and(self.row == 0, self.col == 0)
        self.passer = self.col == jnp.where(self.row == 0, 1, 0)
        self.pass_hi = jnp.where(self.row == 0, pcols - 1, pcols)
        self.has_q = self.col != 0
        self.has_p = self.row != 0

    def up(self, s):
        return lax.rem(self.row + s, self.prows)

    def along(self, s):
        return lax.rem(self.col + s, self.pcols)

    def same_core(self, s):
        return lax.rem(self.col + 2 * s, self.pcols)

    def ready(self):
        barrier = pltpu.get_barrier_semaphore()

        def tell(dev):
            pl.semaphore_signal(barrier, inc=1, device_id=dev, device_id_type=MESH)
        each(1, self.prows, lambda s: tell({"prow": self.up(s)}))

        @pl.when(self.has_p)
        def _():
            each(1, self.pcols, lambda s: tell({"pcol": self.along(s)}))

        @pl.when(jnp.logical_and(self.row == 0, self.col == 1))
        def _():
            tell({"pcol": 0})

        @pl.when(jnp.logical_and(self.row == 0, self.col > 1))
        def _():
            tell({"pcol": 1})
        zero_row = jnp.where(self.col == 0, 1, jnp.where(self.col == 1, self.pcols - 2, 0))
        pl.semaphore_wait(barrier, self.prows - 1 + jnp.where(self.has_p, self.pcols - 1, zero_row))

    def corner(self, ref, half):
        return ref.at[pl.ds(64 * half, 64), pl.ds(0, TB)]

    def part(self, ref, i, part):
        n = HB // self.prows
        top = pl.ds(pl.multiple_of(i * n, n), n)
        low = pl.multiple_of((i // 2) * n, n)
        side = pl.ds(pl.multiple_of(lax.rem(i, 2) * HB, HB), HB)
        if part == 0:
            return ref.at[top, pl.ds(0, HB)]
        if part in (1, 3):
            return ref.at[top, pl.ds(HB + TB * (part // 2), TB)]
        return ref.at[pl.ds(HB + TB * (part // 2 - 1) + low, n), side]

    def corner_out(self, half, s):
        return rcopy(self.corner(self.w, half), self.corner(self.c, half), self.c_send.at[half, s], self.c_recv.at[half],
                     {"prow": self.up(s)})

    def corner_side(self, half):
        return rcopy(self.corner(self.w, half), self.corner(self.c, half), self.cz_send.at[half, 0], self.cz_recv.at[half],
                     {"pcol": 1})

    def corner_on(self, half, s):
        piece = self.corner(self.c, half)
        return rcopy(piece, piece, self.cz_send.at[half, s], self.cz_recv.at[half], {"pcol": self.along(s)})

    def d_out(self, part, s):
        return rcopy(self.part(self.w, self.up(s), part), self.part(self.d, self.up(s), part),
                     self.ds_send.at[part, s], self.ds_recv.at[part], {"prow": self.up(s)})

    def d_side(self, part):
        return rcopy(self.part(self.w, 0, part), self.part(self.d, 0, part),
                     self.dz_send.at[part, 0], self.dz_recv.at[part], {"pcol": 1})

    def d_on(self, part, s):
        piece = self.part(self.d, self.row, part)
        return rcopy(piece, piece, self.dz_send.at[part, s], self.dz_recv.at[part], {"pcol": self.along(s)})

    def d_share(self, part, s):
        piece = self.part(self.d, self.row, part)
        return rcopy(piece, piece, self.da_send.at[part, s], self.da_recv.at[part, self.row], {"prow": self.up(s)})

    def d_from(self, part, s):
        o = self.up(s)
        piece = self.part(self.d, o, part)
        return rcopy(piece, piece, self.da_send.at[part, s], self.da_recv.at[part, o], {"prow": o})

    def own(self, i):
        if i < 2:
            return pltpu.make_async_copy(self.corner(self.w, i), self.corner(self.c, i), self.loc.at[i])
        if i < 2 + PARTS:
            return pltpu.make_async_copy(self.part(self.w, 0, i - 2), self.part(self.d, 0, i - 2), self.loc.at[i])
        if i == OWN_Q:
            return pltpu.make_async_copy(self.q_piece(self.w, 0), self.q_piece(self.q, 0), self.loc.at[i])
        return pltpu.make_async_copy(self.p_piece(self.w, 0), self.p_piece(self.p, 0), self.loc.at[i])

    def q_piece(self, ref, i):
        n = NB // self.prows
        return ref.at[pl.ds(pl.multiple_of(i * n, n), n), :]

    def q_out(self, s):
        o = self.up(s)
        return rcopy(self.q_piece(self.w, o), self.q_piece(self.q, o), self.qs_send.at[s], self.qs_recv, {"prow": o})

    def q_shares(self, fn):
        first = jnp.where(self.row == 0, self.prows, self.prows - self.row)
        each(1, first, lambda s: fn(self.q_share(s)))
        each(first + 1, self.prows, lambda s: fn(self.q_share(s)))

    def q_share(self, s):
        piece = self.q_piece(self.q, self.row)
        return rcopy(piece, piece, self.qa_send.at[s], self.qa_recv.at[self.row], {"prow": self.up(s)})

    def q_from(self, s):
        o = self.up(s)
        piece = self.q_piece(self.q, o)
        return rcopy(piece, piece, self.qa_send.at[s], self.qa_recv.at[o], {"prow": o})

    def p_piece(self, ref, c):
        n = NB // self.pcols
        at = lax.rem(c, 2) * HB + (c // 2) * n
        return ref.at[pl.ds(pl.multiple_of(at, n), n), :]

    def p_half(self, h):
        return self.p.at[pl.ds(pl.multiple_of(h * HB, HB), HB), :]

    def p_out(self, s):
        o = self.along(s)
        return rcopy(self.p_piece(self.w, o), self.p_piece(self.p, o), self.ps_send.at[s], self.ps_recv, {"pcol": o})

    def p_share(self, s):
        piece = self.p_piece(self.p, self.col)
        return rcopy(piece, piece, self.pa_send.at[s], self.pa_recv.at[self.col // 2], {"pcol": self.same_core(s)})

    def p_from(self, s):
        o = self.same_core(s)
        piece = self.p_piece(self.p, o)
        return rcopy(piece, piece, self.pa_send.at[s], self.pa_recv.at[o // 2], {"pcol": o})

    def p_whole(self):
        return rcopy(self.w, self.p, self.px_send, self.px_recv, {"pcol": 1})

    def p_swap(self):
        mine = self.p_half(self.core)
        return rcopy(mine, mine, self.px_send, self.px_recv, {"pcol": self.col + 1 - 2 * self.core})

    def p_swapped(self):
        other = self.p_half(1 - self.core)
        return rcopy(other, other, self.px_send, self.px_recv, {"pcol": self.col + 1 - 2 * self.core})

    def start(self):
        @pl.when(self.root)
        def _():
            self.root_part(0)
            for half in range(2):
                each(1, self.prows, lambda s: self.corner_out(half, s).start())
                self.corner_side(half).start()
                self.own(half).start()
            for part in range(1, PARTS):
                self.root_part(part)

        @pl.when(jnp.logical_and(self.row == 0, self.col > 1))
        def _():
            self.send_q()

        @pl.when(self.passer)
        def _():
            self.pass_part(0)
            for half in range(2):
                @pl.when(self.has_p)
                def _():
                    self.corner_out(half, 0).wait_recv()

                @pl.when(jnp.logical_not(self.has_p))
                def _():
                    self.corner_side(half).wait_recv()
                each(1, self.pass_hi, lambda s: self.corner_on(half, s).start())

    def root_part(self, part):
        each(1, self.prows, lambda s: self.d_out(part, s).start())
        self.d_side(part).start()
        self.own(2 + part).start()

    def pass_part(self, part):
        @pl.when(self.has_p)
        def _():
            self.d_out(part, 0).wait_recv()

        @pl.when(jnp.logical_not(self.has_p))
        def _():
            self.d_side(part).wait_recv()
        each(1, self.pass_hi, lambda s: self.d_on(part, s).start())

    def pass_next(self):
        @pl.when(self.passer)
        def _():
            for part in range(1, 3):
                self.pass_part(part)

            @pl.when(self.has_p)
            def _():
                each(2, self.pcols, lambda s: self.p_out(s).start())
                self.own(OWN_P).start()

    def pass_rest(self):
        @pl.when(self.passer)
        def _():
            for part in range(3, PARTS):
                self.pass_part(part)

            @pl.when(self.has_p)
            def _():
                self.p_whole().start()

            @pl.when(jnp.logical_not(self.has_p))
            def _():
                self.send_q()

    def send_q(self):
        each(1, self.prows, lambda s: self.q_out(s).start())
        self.own(OWN_Q).start()

    def wait_corner(self, half):
        @pl.when(self.root)
        def _():
            self.own(half).wait()

        @pl.when(jnp.logical_not(jnp.logical_or(self.root, self.passer)))
        def _():
            self.corner_on(half, 0).wait_recv()

    def share_d(self, parts):
        for part in parts:
            @pl.when(self.root)
            def _():
                self.own(2 + part).wait()

            @pl.when(jnp.logical_not(jnp.logical_or(self.root, self.passer)))
            def _():
                self.d_on(part, 0).wait_recv()
            each(1, self.prows, lambda s: self.d_share(part, s).start())

    def get_d(self, part):
        each(1, self.prows, lambda s: self.d_from(part, s).wait_recv())

    def share_q(self):
        @pl.when(self.has_q)
        def _():
            @pl.when(self.row == 0)
            def _():
                self.own(OWN_Q).wait()

            @pl.when(self.row != 0)
            def _():
                self.q_out(0).wait_recv()
            self.q_shares(lambda copy: copy.start())

    def get_q(self, q_ref):
        @pl.when(self.row == 0)
        def _():
            q_ref[...] = self.w[...].astype(F32)

        @pl.when(self.row != 0)
        def _():
            each(1, self.prows, lambda s: self.q_from(s).wait_recv())
            q_ref[...] = self.q[...].astype(F32)

    def share_p(self):
        @pl.when(self.has_p)
        def _():
            @pl.when(self.col == 1)
            def _():
                self.p_whole().wait_recv()

            @pl.when(self.col > 1)
            def _():
                self.p_out(0).wait_recv()
            @pl.when(self.col == 0)
            def _():
                self.own(OWN_P).wait()
            self.p_shares(lambda copy: copy.start())

    def p_shares(self, fn):
        chips = self.pcols // 2
        mine = self.col // 2
        each(1, jnp.where(mine == 0, chips, chips - mine), lambda s: fn(self.p_share(s)))
        each(jnp.where(mine == 0, chips, chips - mine + 1), chips, lambda s: fn(self.p_share(s)))

    def swap_p(self):
        @pl.when(self.has_p)
        def _():
            @pl.when(self.col > 1)
            def _():
                each(1, self.pcols // 2, lambda s: self.p_from(s).wait_recv())
                self.p_swap().start()

    def get_p(self, p_ref):
        @pl.when(self.col == 0)
        def _():
            p_ref[...] = self.w[...].astype(F32)

        @pl.when(self.col > 1)
        def _():
            self.p_swapped().wait_recv()

        @pl.when(self.col != 0)
        def _():
            p_ref[...] = self.p[...].astype(F32)

    def finish(self):
        @pl.when(self.root)
        def _():
            for half in range(2):
                each(1, self.prows, lambda s: self.corner_out(half, s).wait_send())
                self.corner_side(half).wait_send()
            for part in range(PARTS):
                each(1, self.prows, lambda s: self.d_out(part, s).wait_send())
                self.d_side(part).wait_send()

        @pl.when(self.passer)
        def _():
            for half in range(2):
                each(1, self.pass_hi, lambda s: self.corner_on(half, s).wait_send())
            for part in range(PARTS):
                each(1, self.pass_hi, lambda s: self.d_on(part, s).wait_send())

            @pl.when(self.has_p)
            def _():
                each(2, self.pcols, lambda s: self.p_out(s).wait_send())
        for part in range(PARTS):
            each(1, self.prows, lambda s: self.d_share(part, s).wait_send())

        @pl.when(self.has_q)
        def _():
            @pl.when(self.row == 0)
            def _():
                each(1, self.prows, lambda s: self.q_out(s).wait_send())
            self.q_shares(lambda copy: copy.wait_send())

        @pl.when(self.has_p)
        def _():
            self.p_shares(lambda copy: copy.wait_send())

            @pl.when(self.col == 0)
            def _():
                self.p_whole().wait_send()

            @pl.when(self.col > 1)
            def _():
                self.p_swap().wait_send()


def step_kernel(prows, pcols, w_hbm, o_ref, w_ref, a_ref, q_ref, p_ref, li_ref, ui_ref, ub_ref, lb_ref,
                c_buf, d_buf, q_buf, p_buf, loc_sem, *sems):
    mv = Moves(prows, pcols, w_ref, c_buf, d_buf, q_buf, p_buf, loc_sem, sems)
    load = pltpu.make_async_copy(w_hbm, w_ref, loc_sem.at[OWN_P + 1])
    load.start()
    mv.ready()
    load.wait()
    mv.start()
    mv.share_d([0])
    mv.wait_corner(0)
    a_ref[0:64, 0:TB] = c_buf[0:64, :].astype(F32)

    def tile_step(k, carry):
        at = pl.ds(pl.multiple_of(k * TB, TB), TB)
        upper = pl.ds(pl.multiple_of(k * TB, 64), 64)
        lower = pl.ds(pl.multiple_of(k * TB + 64, 64), 64)
        top = a_ref[upper, at]
        t0, b0 = leaf(top, 0)

        @pl.when(k == 0)
        def _():
            mv.wait_corner(1)
            a_ref[64:TB, 0:TB] = c_buf[64:TB, :].astype(F32)
            mv.pass_next()

        @pl.when(k == 1)
        def _():
            mv.share_d([3, 4])
            mv.share_q()
            mv.share_p()

        packed, linv, uinv = second_half(t0, b0, top, a_ref[lower, at])
        a_ref[at, at] = packed
        li_ref[k] = linv
        ui_ref[k] = uinv

        @pl.when(k == 0)
        def _():
            mv.pass_rest()
            mv.share_d([1, 2])
            mv.get_d(0)
            a_ref[0:TB, TB:HB] = d_buf[0:TB, TB:HB].astype(F32)
            a_ref[TB:HB, 0:HB] = d_buf[TB:HB, 0:HB].astype(F32)
            strip_update(a_ref, li_ref, ui_ref, 1)

        @pl.when(k == 1)
        def _():
            mv.get_d(1)
            mv.get_d(2)
            a_ref[0:HB, HB:HB + TB] = d_buf[0:HB, HB:HB + TB].astype(F32)
            a_ref[HB:HB + TB, 0:HB + TB] = d_buf[HB:HB + TB, 0:HB + TB].astype(F32)
            strip_update(a_ref, li_ref, ui_ref, 2)

        @pl.when(k == 2)
        def _():
            mv.get_d(3)
            mv.get_d(4)
            mv.swap_p()
            a_ref[0:HB + TB, HB + TB:NB] = d_buf[0:HB + TB, HB + TB:NB].astype(F32)
            a_ref[HB + TB:NB, :] = d_buf[HB + TB:NB, :].astype(F32)
            strip_update(a_ref, li_ref, ui_ref, 3)
        return carry

    lax.fori_loop(0, 4, tile_step, 0)

    @pl.when(mv.has_q)
    def _():
        mv.get_q(q_ref)

    @pl.when(mv.has_p)
    def _():
        mv.get_p(p_ref)

    @pl.when(jnp.logical_and(mv.has_p, mv.has_q))
    def _():
        for j in range(4):
            solve_u(a_ref, li_ref, q_ref, ub_ref, j)
            solve_l(a_ref, ui_ref, p_ref, lb_ref, j)
        o_ref[...] = (w_ref[...].astype(F32) - dot(lb_ref[...], ub_ref[...])).astype(BF)

    @pl.when(jnp.logical_and(jnp.logical_not(mv.has_p), mv.has_q))
    def _():
        for j in range(4):
            solve_u(a_ref, li_ref, q_ref, ub_ref, j)
        o_ref[...] = ub_ref[...]

    @pl.when(jnp.logical_and(mv.has_p, jnp.logical_not(mv.has_q)))
    def _():
        for j in range(4):
            solve_l(a_ref, ui_ref, p_ref, lb_ref, j)
        o_ref[...] = lb_ref[...]

    @pl.when(mv.root)
    def _():
        o_ref[...] = a_ref[...].astype(BF)

    mv.finish()


def per_device(matrix):
    prows, pcols = lax.axis_size("prow"), lax.axis_size("pcol")
    dma = pltpu.SemaphoreType.DMA
    out = pl.pallas_call(
        functools.partial(step_kernel, prows, pcols),
        out_shape=pltpu.VMEM((NB, NB), BF),
        in_specs=[pl.BlockSpec(memory_space=pl.ANY)],
        out_specs=pl.BlockSpec(memory_space=pltpu.VMEM),
        scratch_shapes=[
            pltpu.VMEM((NB, NB), BF),
            pltpu.VMEM((NB, NB), F32), pltpu.VMEM((NB, NB), F32), pltpu.VMEM((NB, NB), F32),
            pltpu.VMEM((4, TB, TB), F32), pltpu.VMEM((4, TB, TB), F32),
            pltpu.VMEM((NB, NB), BF), pltpu.VMEM((NB, NB), BF),
            pltpu.VMEM((TB, TB), BF), pltpu.VMEM((NB, NB), BF), pltpu.VMEM((NB, NB), BF), pltpu.VMEM((NB, NB), BF),
            dma((5 + PARTS,)),
            dma((2, prows)), dma((2,)), dma((2, pcols)), dma((2,)),
            dma((PARTS, prows)), dma((PARTS,)), dma((PARTS, pcols)), dma((PARTS,)), dma((PARTS, prows)), dma((PARTS, prows)),
            dma((prows,)), dma, dma((prows,)), dma((prows,)),
            dma((pcols,)), dma, dma((pcols // 2,)), dma((pcols // 2,)), dma, dma,
        ],
        compiler_params=pltpu.CompilerParams(collective_id=0, has_side_effects=True),
    )(matrix.reshape(NB, NB))
    return out.reshape(matrix.shape)


def solution(mesh):
    placed = P(None, "prow", None, "pcol")
    return jax.shard_map(per_device, mesh=mesh, in_specs=(placed,), out_specs=placed, check_vma=False)
```

```python
import functools

import jax
import jax.numpy as jnp
from jax import lax
from jax.experimental import pallas as pl
from jax.experimental.pallas import tpu as pltpu
from jax.sharding import PartitionSpec as P

F32 = jnp.float32
BF = jnp.bfloat16
NB = 512
HB = 256
TB = 128
PARTS = 5
OWN_Q, OWN_P = 2 + PARTS, 3 + PARTS
MESH = pl.DeviceIdType.MESH


def split(x):
    hi = x.astype(BF)
    lo = (x - hi.astype(F32)).astype(BF)
    return hi, lo

def dot(a, b):
    return jnp.dot(a, b, preferred_element_type=F32)

def dot3s(a, b):
    ah, al = a; bh, bl = b
    return dot(jnp.concatenate([ah, al, ah], 1), jnp.concatenate([bh, bh, bl], 0))

def dot3(a, b):
    return dot3s(split(a), split(b))

def iotas(rows=8):
    return (lax.broadcasted_iota(jnp.int32, (rows, 128), 0), lax.broadcasted_iota(jnp.int32, (rows, 128), 1))

def leaf(block, base):
    sub, lane = iotas()
    other = 64 - base
    tiles = []
    for t in range(8):
        eye = jnp.where(lane == other + 8 * t + sub, 1.0, 0.0)
        keep = (lane >= base) & (lane < base + 64)
        tiles.append(jnp.where(keep, block[8 * t:8 * t + 8, :], eye))
    low = [None] * 8
    for g in range(8):
        c0 = base + 8 * g
        inside = (lane >= c0) & (lane < c0 + 8)
        grp = tiles[g]
        cols = [jnp.broadcast_to(grp[:, c0 + j:c0 + j + 1], (8, 128)) for j in range(8)]
        outer = {}
        for t in list(range(g + 1, 8)) + [8 + s for s in range(g)]:
            src = tiles[t] if t < 8 else low[t - 8]
            outer[t] = [jnp.broadcast_to(src[:, c0 + j:c0 + j + 1], (8, 128)) for j in range(8)]
        done = (lane >= base) & (lane < c0)
        held = grp
        grp = jnp.where(done, 0.0, grp)
        mult = jnp.zeros((8, 128), F32)
        v = jnp.where(inside, jnp.where(lane == c0 + sub, 1.0, 0.0), grp)
        scale = jnp.zeros((8, 128), F32)
        for j in range(8):
            piv = jnp.broadcast_to(cols[j][j:j + 1, :], (8, 128))
            rcp = 1.0 / piv
            m = jnp.where(sub == j, 0.0, cols[j] * rcp)
            for i in range(j + 1, 8):
                cols[i] = cols[i] - m * jnp.broadcast_to(cols[i][j:j + 1, :], (8, 128))
            mlow = jnp.where(sub > j, m, 0.0)
            grp = grp - mlow * jnp.broadcast_to(grp[j:j + 1, :], (8, 128))
            mult = jnp.where(lane == c0 + j, m, mult)
            mv = jnp.where(inside & (sub > j), 0.0, m)
            v = v - mv * jnp.broadcast_to(v[j:j + 1, :], (8, 128))
            scale = jnp.where(sub == j, rcp, scale)
        grp = jnp.where(inside & (lane < c0 + sub), mult, grp)
        tiles[g] = jnp.where(done, held, grp)
        v = v * scale
        v = jnp.where(inside, -v, v)
        rows = [jnp.broadcast_to(v[j:j + 1, :], (8, 128)) for j in range(8)]
        for t, cs in outer.items():
            src = tiles[t] if t < 8 else low[t - 8]
            p = [cs[j] * rows[j] for j in range(8)]
            tot = ((p[0] + p[1]) + (p[2] + p[3])) + ((p[4] + p[5]) + (p[6] + p[7]))
            new = jnp.where(inside, 0.0, src) - tot
            if t < 8:
                tiles[t] = new
            else:
                low[t - 8] = new
        low[g] = -v
    return jnp.concatenate(tiles, 0), jnp.concatenate(low, 0)


def second_half(t0, b0, top, bot):
    _, lane = iotas(64)
    left = lane < 64
    z = jnp.zeros((64, 128), F32)
    linv0 = jnp.where(left, 0.0, t0)
    uinv0 = jnp.where(left, b0, 0.0)
    u01 = jnp.where(left, 0.0, dot3(linv0, jnp.concatenate([z, top], 0)))
    l10 = dot3(jnp.where(left, bot, 0.0), jnp.concatenate([uinv0, z], 0))
    sch = bot - dot3(l10, jnp.concatenate([u01, z], 0))
    t1, b1 = leaf(sch, 64)
    linv0r = pltpu.roll(linv0, 64, 1)
    zl = dot3(l10, jnp.concatenate([linv0r, z], 0))
    zu = dot3(uinv0, jnp.concatenate([u01, z], 0))
    linv1 = jnp.where(left, t1, 0.0)
    uinv1 = jnp.where(left, 0.0, b1)
    linv10 = dot3(linv1, jnp.concatenate([zl, z], 0))
    uinv01 = dot3(zu, jnp.concatenate([z, uinv1], 0))
    packed = jnp.concatenate([jnp.where(left, t0, u01), jnp.where(left, l10, t1)], 0)
    linv = jnp.concatenate([linv0r, pltpu.roll(linv1, 64, 1) - linv10], 0)
    uinv = jnp.concatenate([uinv0 - uinv01, uinv1], 0)
    return packed, linv, uinv


def blk(i):
    return slice(TB * i, TB * (i + 1))


def later(i):
    return slice(TB * (i + 1), NB)


def strip_update(a_ref, li_ref, ui_ref, n):
    us, ls = [], []
    for i in range(n):
        u = a_ref[blk(i), blk(n)]
        l = a_ref[blk(n), blk(i)]
        for j in range(i):
            u = u - dot3(a_ref[blk(i), blk(j)], us[j])
            l = l - dot3(ls[j], a_ref[blk(j), blk(i)])
        us.append(dot3(li_ref[i], u))
        ls.append(dot3(l, ui_ref[i]))
    schur = a_ref[blk(n), blk(n)]
    for u, l in zip(us, ls):
        schur = schur - dot3(l, u)
    for i in range(n):
        a_ref[blk(i), blk(n)] = us[i]
        a_ref[blk(n), blk(i)] = ls[i]
    a_ref[blk(n), blk(n)] = schur


def solve_u(a_ref, li_ref, q_ref, ub_ref, j):
    u = dot3(li_ref[j], q_ref[blk(j), :])
    ub_ref[blk(j), :] = u.astype(BF)
    if j < 3:
        q_ref[later(j), :] = q_ref[later(j), :] - dot3(a_ref[later(j), blk(j)], u)


def solve_l(a_ref, ui_ref, p_ref, lb_ref, j):
    l = dot3(p_ref[:, blk(j)], ui_ref[j])
    lb_ref[:, blk(j)] = l.astype(BF)
    if j < 3:
        p_ref[:, later(j)] = p_ref[:, later(j)] - dot3(l, a_ref[blk(j), later(j)])


def rcopy(src, dst, ss, rs, dev):
    return pltpu.make_async_remote_copy(src_ref=src, dst_ref=dst, send_sem=ss, recv_sem=rs,
                                        device_id=dev, device_id_type=MESH)


def each(lo, hi, fn):
    def one(s, carry):
        fn(s)
        return carry
    lax.fori_loop(lo, hi, one, 0)


class Moves:
    def __init__(self, prows, pcols, w_ref, c_buf, d_buf, q_buf, p_buf, loc_sem, sems):
        self.prows, self.pcols = prows, pcols
        self.row, self.col = lax.axis_index("prow"), lax.axis_index("pcol")
        self.core = lax.rem(self.col, 2)
        self.w, self.c, self.d, self.q, self.p = w_ref, c_buf, d_buf, q_buf, p_buf
        self.loc = loc_sem
        (self.c_send, self.c_recv, self.cz_send, self.cz_recv,
         self.ds_send, self.ds_recv, self.dz_send, self.dz_recv, self.da_send, self.da_recv,
         self.qs_send, self.qs_recv, self.qa_send, self.qa_recv,
         self.ps_send, self.ps_recv, self.pa_send, self.pa_recv, self.px_send, self.px_recv) = sems
        self.root = jnp.logical_and(self.row == 0, self.col == 0)
        self.passer = self.col == jnp.where(self.row == 0, 1, 0)
        self.pass_hi = jnp.where(self.row == 0, pcols - 1, pcols)
        self.has_q = self.col != 0
        self.has_p = self.row != 0

    def up(self, s):
        return lax.rem(self.row + jnp.where(self.core == 0, s, self.prows - s), self.prows)

    def along(self, s):
        return lax.rem(self.col + s, self.pcols)

    def same_core(self, s):
        return lax.rem(self.col + 2 * s, self.pcols)

    def ready(self):
        barrier = pltpu.get_barrier_semaphore()

        def tell(dev):
            pl.semaphore_signal(barrier, inc=1, device_id=dev, device_id_type=MESH)
        each(1, self.prows, lambda s: tell({"prow": self.up(s)}))

        @pl.when(self.has_p)
        def _():
            each(1, self.pcols, lambda s: tell({"pcol": self.along(s)}))

        @pl.when(jnp.logical_and(self.row == 0, self.col == 1))
        def _():
            tell({"pcol": 0})

        @pl.when(jnp.logical_and(self.row == 0, self.col > 1))
        def _():
            tell({"pcol": 1})
        zero_row = jnp.where(self.col == 0, 1, jnp.where(self.col == 1, self.pcols - 2, 0))
        pl.semaphore_wait(barrier, self.prows - 1 + jnp.where(self.has_p, self.pcols - 1, zero_row))

    def corner(self, ref, half):
        return ref.at[pl.ds(64 * half, 64), pl.ds(0, TB)]

    def part(self, ref, i, part):
        n = HB // self.prows
        top = pl.ds(pl.multiple_of(i * n, n), n)
        low = pl.multiple_of((i // 2) * n, n)
        side = pl.ds(pl.multiple_of(lax.rem(i, 2) * HB, HB), HB)
        if part == 0:
            return ref.at[top, pl.ds(0, HB)]
        if part in (1, 3):
            return ref.at[top, pl.ds(HB + TB * (part // 2), TB)]
        return ref.at[pl.ds(HB + TB * (part // 2 - 1) + low, n), side]

    def corner_out(self, half, s):
        return rcopy(self.corner(self.w, half), self.corner(self.c, half), self.c_send.at[half, s], self.c_recv.at[half],
                     {"prow": self.up(s)})

    def corner_side(self, half):
        return rcopy(self.corner(self.w, half), self.corner(self.c, half), self.cz_send.at[half, 0], self.cz_recv.at[half],
                     {"pcol": 1})

    def corner_on(self, half, s):
        piece = self.corner(self.c, half)
        return rcopy(piece, piece, self.cz_send.at[half, s], self.cz_recv.at[half], {"pcol": self.along(s)})

    def d_out(self, part, s):
        return rcopy(self.part(self.w, self.up(s), part), self.part(self.d, self.up(s), part),
                     self.ds_send.at[part, s], self.ds_recv.at[part], {"prow": self.up(s)})

    def d_side(self, part):
        return rcopy(self.part(self.w, 0, part), self.part(self.d, 0, part),
                     self.dz_send.at[part, 0], self.dz_recv.at[part], {"pcol": 1})

    def d_on(self, part, s):
        piece = self.part(self.d, self.row, part)
        return rcopy(piece, piece, self.dz_send.at[part, s], self.dz_recv.at[part], {"pcol": self.along(s)})

    def d_share(self, part, s):
        piece = self.part(self.d, self.row, part)
        return rcopy(piece, piece, self.da_send.at[part, s], self.da_recv.at[part, self.row], {"prow": self.up(s)})

    def d_from(self, part, s):
        o = self.up(s)
        piece = self.part(self.d, o, part)
        return rcopy(piece, piece, self.da_send.at[part, s], self.da_recv.at[part, o], {"prow": o})

    def own(self, i):
        if i < 2:
            return pltpu.make_async_copy(self.corner(self.w, i), self.corner(self.c, i), self.loc.at[i])
        if i < 2 + PARTS:
            return pltpu.make_async_copy(self.part(self.w, 0, i - 2), self.part(self.d, 0, i - 2), self.loc.at[i])
        if i == OWN_Q:
            return pltpu.make_async_copy(self.q_piece(self.w, 0), self.q_piece(self.q, 0), self.loc.at[i])
        return pltpu.make_async_copy(self.p_piece(self.w, 0), self.p_piece(self.p, 0), self.loc.at[i])

    def q_piece(self, ref, i):
        n = NB // self.prows
        return ref.at[pl.ds(pl.multiple_of(i * n, n), n), :]

    def q_out(self, s):
        o = self.up(s)
        return rcopy(self.q_piece(self.w, o), self.q_piece(self.q, o), self.qs_send.at[s], self.qs_recv, {"prow": o})

    def q_shares(self, fn):
        first = jnp.where(self.row == 0, self.prows, jnp.where(self.core == 0, self.prows - self.row, self.row))
        each(1, first, lambda s: fn(self.q_share(s)))
        each(first + 1, self.prows, lambda s: fn(self.q_share(s)))

    def q_share(self, s):
        piece = self.q_piece(self.q, self.row)
        return rcopy(piece, piece, self.qa_send.at[s], self.qa_recv.at[self.row], {"prow": self.up(s)})

    def q_from(self, s):
        o = self.up(s)
        piece = self.q_piece(self.q, o)
        return rcopy(piece, piece, self.qa_send.at[s], self.qa_recv.at[o], {"prow": o})

    def p_piece(self, ref, c):
        n = NB // self.pcols
        at = lax.rem(c, 2) * HB + (c // 2) * n
        return ref.at[pl.ds(pl.multiple_of(at, n), n), :]

    def p_half(self, h):
        return self.p.at[pl.ds(pl.multiple_of(h * HB, HB), HB), :]

    def p_out(self, s):
        o = self.along(s)
        return rcopy(self.p_piece(self.w, o), self.p_piece(self.p, o), self.ps_send.at[s], self.ps_recv, {"pcol": o})

    def p_share(self, s):
        piece = self.p_piece(self.p, self.col)
        return rcopy(piece, piece, self.pa_send.at[s], self.pa_recv.at[self.col // 2], {"pcol": self.same_core(s)})

    def p_from(self, s):
        o = self.same_core(s)
        piece = self.p_piece(self.p, o)
        return rcopy(piece, piece, self.pa_send.at[s], self.pa_recv.at[o // 2], {"pcol": o})

    def p_whole(self):
        return rcopy(self.w, self.p, self.px_send, self.px_recv, {"pcol": 1})

    def p_swap(self):
        mine = self.p_half(self.core)
        return rcopy(mine, mine, self.px_send, self.px_recv, {"pcol": self.col + 1 - 2 * self.core})

    def p_swapped(self):
        other = self.p_half(1 - self.core)
        return rcopy(other, other, self.px_send, self.px_recv, {"pcol": self.col + 1 - 2 * self.core})

    def start(self):
        @pl.when(self.root)
        def _():
            self.root_part(0)
            for half in range(2):
                each(1, self.prows, lambda s: self.corner_out(half, s).start())
                self.corner_side(half).start()
                self.own(half).start()
            for part in range(1, PARTS):
                self.root_part(part)

        @pl.when(jnp.logical_and(self.row == 0, self.col > 1))
        def _():
            self.send_q()

        @pl.when(self.passer)
        def _():
            self.pass_part(0)
            for half in range(2):
                @pl.when(self.has_p)
                def _():
                    self.corner_out(half, 0).wait_recv()

                @pl.when(jnp.logical_not(self.has_p))
                def _():
                    self.corner_side(half).wait_recv()
                each(1, self.pass_hi, lambda s: self.corner_on(half, s).start())

    def root_part(self, part):
        each(1, self.prows, lambda s: self.d_out(part, s).start())
        self.d_side(part).start()
        self.own(2 + part).start()

    def pass_part(self, part):
        @pl.when(self.has_p)
        def _():
            self.d_out(part, 0).wait_recv()

        @pl.when(jnp.logical_not(self.has_p))
        def _():
            self.d_side(part).wait_recv()
        each(1, self.pass_hi, lambda s: self.d_on(part, s).start())

    def pass_next(self):
        @pl.when(self.passer)
        def _():
            for part in range(1, 3):
                self.pass_part(part)

            @pl.when(self.has_p)
            def _():
                each(2, self.pcols, lambda s: self.p_out(s).start())
                self.own(OWN_P).start()

    def pass_rest(self):
        @pl.when(self.passer)
        def _():
            for part in range(3, PARTS):
                self.pass_part(part)

            @pl.when(self.has_p)
            def _():
                self.p_whole().start()

            @pl.when(jnp.logical_not(self.has_p))
            def _():
                self.send_q()

    def send_q(self):
        each(1, self.prows, lambda s: self.q_out(s).start())
        self.own(OWN_Q).start()

    def wait_corner(self, half):
        @pl.when(self.root)
        def _():
            self.own(half).wait()

        @pl.when(jnp.logical_not(jnp.logical_or(self.root, self.passer)))
        def _():
            self.corner_on(half, 0).wait_recv()

    def share_d(self, parts):
        for part in parts:
            @pl.when(self.root)
            def _():
                self.own(2 + part).wait()

            @pl.when(jnp.logical_not(jnp.logical_or(self.root, self.passer)))
            def _():
                self.d_on(part, 0).wait_recv()
            each(1, self.prows, lambda s: self.d_share(part, s).start())

    def get_d(self, part):
        each(1, self.prows, lambda s: self.d_from(part, s).wait_recv())

    def share_q(self):
        @pl.when(self.has_q)
        def _():
            @pl.when(self.row == 0)
            def _():
                self.own(OWN_Q).wait()

            @pl.when(self.row != 0)
            def _():
                self.q_out(0).wait_recv()
            self.q_shares(lambda copy: copy.start())

    def get_q(self, q_ref):
        @pl.when(self.row == 0)
        def _():
            q_ref[...] = self.w[...].astype(F32)

        @pl.when(self.row != 0)
        def _():
            each(1, self.prows, lambda s: self.q_from(s).wait_recv())
            q_ref[...] = self.q[...].astype(F32)

    def share_p(self):
        @pl.when(self.has_p)
        def _():
            @pl.when(self.col == 1)
            def _():
                self.p_whole().wait_recv()

            @pl.when(self.col > 1)
            def _():
                self.p_out(0).wait_recv()
            @pl.when(self.col == 0)
            def _():
                self.own(OWN_P).wait()
            self.p_shares(lambda copy: copy.start())

    def p_shares(self, fn):
        chips = self.pcols // 2
        mine = self.col // 2
        each(1, jnp.where(mine == 0, chips, chips - mine), lambda s: fn(self.p_share(s)))
        each(jnp.where(mine == 0, chips, chips - mine + 1), chips, lambda s: fn(self.p_share(s)))

    def swap_p(self):
        @pl.when(self.has_p)
        def _():
            @pl.when(self.col > 1)
            def _():
                each(1, self.pcols // 2, lambda s: self.p_from(s).wait_recv())
                self.p_swap().start()

    def get_p(self, p_ref):
        @pl.when(self.col == 0)
        def _():
            p_ref[...] = self.w[...].astype(F32)

        @pl.when(self.col > 1)
        def _():
            self.p_swapped().wait_recv()

        @pl.when(self.col != 0)
        def _():
            p_ref[...] = self.p[...].astype(F32)

    def finish(self):
        @pl.when(self.root)
        def _():
            for half in range(2):
                each(1, self.prows, lambda s: self.corner_out(half, s).wait_send())
                self.corner_side(half).wait_send()
            for part in range(PARTS):
                each(1, self.prows, lambda s: self.d_out(part, s).wait_send())
                self.d_side(part).wait_send()

        @pl.when(self.passer)
        def _():
            for half in range(2):
                each(1, self.pass_hi, lambda s: self.corner_on(half, s).wait_send())
            for part in range(PARTS):
                each(1, self.pass_hi, lambda s: self.d_on(part, s).wait_send())

            @pl.when(self.has_p)
            def _():
                each(2, self.pcols, lambda s: self.p_out(s).wait_send())
        for part in range(PARTS):
            each(1, self.prows, lambda s: self.d_share(part, s).wait_send())

        @pl.when(self.has_q)
        def _():
            @pl.when(self.row == 0)
            def _():
                each(1, self.prows, lambda s: self.q_out(s).wait_send())
            self.q_shares(lambda copy: copy.wait_send())

        @pl.when(self.has_p)
        def _():
            self.p_shares(lambda copy: copy.wait_send())

            @pl.when(self.col == 0)
            def _():
                self.p_whole().wait_send()

            @pl.when(self.col > 1)
            def _():
                self.p_swap().wait_send()


def step_kernel(prows, pcols, w_hbm, o_ref, w_ref, a_ref, q_ref, p_ref, li_ref, ui_ref, ub_ref, lb_ref,
                c_buf, d_buf, q_buf, p_buf, loc_sem, *sems):
    mv = Moves(prows, pcols, w_ref, c_buf, d_buf, q_buf, p_buf, loc_sem, sems)
    load = pltpu.make_async_copy(w_hbm, w_ref, loc_sem.at[OWN_P + 1])
    load.start()
    mv.ready()
    load.wait()
    mv.start()
    mv.share_d([0])
    mv.wait_corner(0)
    a_ref[0:64, 0:TB] = c_buf[0:64, :].astype(F32)

    def tile_step(k, carry):
        at = pl.ds(pl.multiple_of(k * TB, TB), TB)
        upper = pl.ds(pl.multiple_of(k * TB, 64), 64)
        lower = pl.ds(pl.multiple_of(k * TB + 64, 64), 64)
        top = a_ref[upper, at]
        t0, b0 = leaf(top, 0)

        @pl.when(k == 0)
        def _():
            mv.wait_corner(1)
            a_ref[64:TB, 0:TB] = c_buf[64:TB, :].astype(F32)
            mv.pass_next()

        @pl.when(k == 1)
        def _():
            mv.share_d([3, 4])
            mv.share_q()
            mv.share_p()

        packed, linv, uinv = second_half(t0, b0, top, a_ref[lower, at])
        a_ref[at, at] = packed
        li_ref[k] = linv
        ui_ref[k] = uinv

        @pl.when(k == 0)
        def _():
            mv.pass_rest()
            mv.share_d([1, 2])
            mv.get_d(0)
            a_ref[0:TB, TB:HB] = d_buf[0:TB, TB:HB].astype(F32)
            a_ref[TB:HB, 0:HB] = d_buf[TB:HB, 0:HB].astype(F32)
            strip_update(a_ref, li_ref, ui_ref, 1)

        @pl.when(k == 1)
        def _():
            mv.get_d(1)
            mv.get_d(2)
            a_ref[0:HB, HB:HB + TB] = d_buf[0:HB, HB:HB + TB].astype(F32)
            a_ref[HB:HB + TB, 0:HB + TB] = d_buf[HB:HB + TB, 0:HB + TB].astype(F32)
            strip_update(a_ref, li_ref, ui_ref, 2)

        @pl.when(k == 2)
        def _():
            mv.get_d(3)
            mv.get_d(4)
            mv.swap_p()
            a_ref[0:HB + TB, HB + TB:NB] = d_buf[0:HB + TB, HB + TB:NB].astype(F32)
            a_ref[HB + TB:NB, :] = d_buf[HB + TB:NB, :].astype(F32)
            strip_update(a_ref, li_ref, ui_ref, 3)
        return carry

    lax.fori_loop(0, 4, tile_step, 0)

    @pl.when(mv.has_q)
    def _():
        mv.get_q(q_ref)

    @pl.when(mv.has_p)
    def _():
        mv.get_p(p_ref)

    @pl.when(jnp.logical_and(mv.has_p, mv.has_q))
    def _():
        for j in range(4):
            solve_u(a_ref, li_ref, q_ref, ub_ref, j)
            solve_l(a_ref, ui_ref, p_ref, lb_ref, j)
        o_ref[...] = (w_ref[...].astype(F32) - dot(lb_ref[...], ub_ref[...])).astype(BF)

    @pl.when(jnp.logical_and(jnp.logical_not(mv.has_p), mv.has_q))
    def _():
        for j in range(4):
            solve_u(a_ref, li_ref, q_ref, ub_ref, j)
        o_ref[...] = ub_ref[...]

    @pl.when(jnp.logical_and(mv.has_p, jnp.logical_not(mv.has_q)))
    def _():
        for j in range(4):
            solve_l(a_ref, ui_ref, p_ref, lb_ref, j)
        o_ref[...] = lb_ref[...]

    @pl.when(mv.root)
    def _():
        o_ref[...] = a_ref[...].astype(BF)

    mv.finish()


def per_device(matrix):
    prows, pcols = lax.axis_size("prow"), lax.axis_size("pcol")
    dma = pltpu.SemaphoreType.DMA
    out = pl.pallas_call(
        functools.partial(step_kernel, prows, pcols),
        out_shape=pltpu.VMEM((NB, NB), BF),
        in_specs=[pl.BlockSpec(memory_space=pl.ANY)],
        out_specs=pl.BlockSpec(memory_space=pltpu.VMEM),
        scratch_shapes=[
            pltpu.VMEM((NB, NB), BF),
            pltpu.VMEM((NB, NB), F32), pltpu.VMEM((NB, NB), F32), pltpu.VMEM((NB, NB), F32),
            pltpu.VMEM((4, TB, TB), F32), pltpu.VMEM((4, TB, TB), F32),
            pltpu.VMEM((NB, NB), BF), pltpu.VMEM((NB, NB), BF),
            pltpu.VMEM((TB, TB), BF), pltpu.VMEM((NB, NB), BF), pltpu.VMEM((NB, NB), BF), pltpu.VMEM((NB, NB), BF),
            dma((5 + PARTS,)),
            dma((2, prows)), dma((2,)), dma((2, pcols)), dma((2,)),
            dma((PARTS, prows)), dma((PARTS,)), dma((PARTS, pcols)), dma((PARTS,)), dma((PARTS, prows)), dma((PARTS, prows)),
            dma((prows,)), dma, dma((prows,)), dma((prows,)),
            dma((pcols,)), dma, dma((pcols // 2,)), dma((pcols // 2,)), dma, dma,
        ],
        compiler_params=pltpu.CompilerParams(collective_id=0, has_side_effects=True),
    )(matrix.reshape(NB, NB))
    return out.reshape(matrix.shape)


def solution(mesh):
    placed = P(None, "prow", None, "pcol")
    return jax.shard_map(per_device, mesh=mesh, in_specs=(placed,), out_specs=placed, check_vma=False)
```

```python
import functools

import jax
import jax.numpy as jnp
from jax import lax
from jax.experimental import pallas as pl
from jax.experimental.pallas import tpu as pltpu
from jax.sharding import PartitionSpec as P

F32 = jnp.float32
BF = jnp.bfloat16
NB = 512
HB = 256
TB = 128
PARTS = 5
OWN_Q, OWN_P = 2 + PARTS, 3 + PARTS
MESH = pl.DeviceIdType.MESH


def split(x):
    hi = x.astype(BF)
    lo = (x - hi.astype(F32)).astype(BF)
    return hi, lo

def dot(a, b):
    return jnp.dot(a, b, preferred_element_type=F32)

def dot3s(a, b):
    ah, al = a; bh, bl = b
    return dot(jnp.concatenate([ah, al, ah], 1), jnp.concatenate([bh, bh, bl], 0))

def dot3(a, b):
    return dot3s(split(a), split(b))

def iotas(rows=8):
    return (lax.broadcasted_iota(jnp.int32, (rows, 128), 0), lax.broadcasted_iota(jnp.int32, (rows, 128), 1))

def leaf(block, base):
    sub, lane = iotas()
    other = 64 - base
    tiles = []
    for t in range(8):
        eye = jnp.where(lane == other + 8 * t + sub, 1.0, 0.0)
        keep = (lane >= base) & (lane < base + 64)
        tiles.append(jnp.where(keep, block[8 * t:8 * t + 8, :], eye))
    low = [None] * 8
    for g in range(8):
        c0 = base + 8 * g
        inside = (lane >= c0) & (lane < c0 + 8)
        grp = tiles[g]
        cols = [jnp.broadcast_to(grp[:, c0 + j:c0 + j + 1], (8, 128)) for j in range(8)]
        outer = {}
        for t in list(range(g + 1, 8)) + [8 + s for s in range(g)]:
            src = tiles[t] if t < 8 else low[t - 8]
            outer[t] = [jnp.broadcast_to(src[:, c0 + j:c0 + j + 1], (8, 128)) for j in range(8)]
        done = (lane >= base) & (lane < c0)
        held = grp
        grp = jnp.where(done, 0.0, grp)
        mult = jnp.zeros((8, 128), F32)
        v = jnp.where(inside, jnp.where(lane == c0 + sub, 1.0, 0.0), grp)
        scale = jnp.zeros((8, 128), F32)
        for j in range(8):
            piv = jnp.broadcast_to(cols[j][j:j + 1, :], (8, 128))
            rcp = 1.0 / piv
            m = jnp.where(sub == j, 0.0, cols[j] * rcp)
            for i in range(j + 1, 8):
                cols[i] = cols[i] - m * jnp.broadcast_to(cols[i][j:j + 1, :], (8, 128))
            mlow = jnp.where(sub > j, m, 0.0)
            grp = grp - mlow * jnp.broadcast_to(grp[j:j + 1, :], (8, 128))
            mult = jnp.where(lane == c0 + j, m, mult)
            mv = jnp.where(inside & (sub > j), 0.0, m)
            v = v - mv * jnp.broadcast_to(v[j:j + 1, :], (8, 128))
            scale = jnp.where(sub == j, rcp, scale)
        grp = jnp.where(inside & (lane < c0 + sub), mult, grp)
        tiles[g] = jnp.where(done, held, grp)
        v = v * scale
        v = jnp.where(inside, -v, v)
        rows = [jnp.broadcast_to(v[j:j + 1, :], (8, 128)) for j in range(8)]
        for t, cs in outer.items():
            src = tiles[t] if t < 8 else low[t - 8]
            p = [cs[j] * rows[j] for j in range(8)]
            tot = ((p[0] + p[1]) + (p[2] + p[3])) + ((p[4] + p[5]) + (p[6] + p[7]))
            new = jnp.where(inside, 0.0, src) - tot
            if t < 8:
                tiles[t] = new
            else:
                low[t - 8] = new
        low[g] = -v
    return jnp.concatenate(tiles, 0), jnp.concatenate(low, 0)


def second_half(t0, b0, top, bot):
    _, lane = iotas(64)
    left = lane < 64
    z = jnp.zeros((64, 128), F32)
    linv0 = jnp.where(left, 0.0, t0)
    uinv0 = jnp.where(left, b0, 0.0)
    u01 = jnp.where(left, 0.0, dot3(linv0, jnp.concatenate([z, top], 0)))
    l10 = dot3(jnp.where(left, bot, 0.0), jnp.concatenate([uinv0, z], 0))
    sch = bot - dot3(l10, jnp.concatenate([u01, z], 0))
    t1, b1 = leaf(sch, 64)
    linv0r = pltpu.roll(linv0, 64, 1)
    zl = dot3(l10, jnp.concatenate([linv0r, z], 0))
    zu = dot3(uinv0, jnp.concatenate([u01, z], 0))
    linv1 = jnp.where(left, t1, 0.0)
    uinv1 = jnp.where(left, 0.0, b1)
    linv10 = dot3(linv1, jnp.concatenate([zl, z], 0))
    uinv01 = dot3(zu, jnp.concatenate([z, uinv1], 0))
    packed = jnp.concatenate([jnp.where(left, t0, u01), jnp.where(left, l10, t1)], 0)
    linv = jnp.concatenate([linv0r, pltpu.roll(linv1, 64, 1) - linv10], 0)
    uinv = jnp.concatenate([uinv0 - uinv01, uinv1], 0)
    return packed, linv, uinv


def blk(i):
    return slice(TB * i, TB * (i + 1))


def later(i):
    return slice(TB * (i + 1), NB)


def strip_update(a_ref, li_ref, ui_ref, n):
    us, ls = [], []
    for i in range(n):
        u = a_ref[blk(i), blk(n)]
        l = a_ref[blk(n), blk(i)]
        for j in range(i):
            u = u - dot3(a_ref[blk(i), blk(j)], us[j])
            l = l - dot3(ls[j], a_ref[blk(j), blk(i)])
        us.append(dot3(li_ref[i], u))
        ls.append(dot3(l, ui_ref[i]))
    schur = a_ref[blk(n), blk(n)]
    for u, l in zip(us, ls):
        schur = schur - dot3(l, u)
    for i in range(n):
        a_ref[blk(i), blk(n)] = us[i]
        a_ref[blk(n), blk(i)] = ls[i]
    a_ref[blk(n), blk(n)] = schur


def solve_u(a_ref, li_ref, q_ref, ub_ref, j):
    u = dot3(li_ref[j], q_ref[blk(j), :])
    ub_ref[blk(j), :] = u.astype(BF)
    if j < 3:
        q_ref[later(j), :] = q_ref[later(j), :] - dot3(a_ref[later(j), blk(j)], u)


def solve_l(a_ref, ui_ref, p_ref, lb_ref, j):
    l = dot3(p_ref[:, blk(j)], ui_ref[j])
    lb_ref[:, blk(j)] = l.astype(BF)
    if j < 3:
        p_ref[:, later(j)] = p_ref[:, later(j)] - dot3(l, a_ref[blk(j), later(j)])


def rcopy(src, dst, ss, rs, dev):
    return pltpu.make_async_remote_copy(src_ref=src, dst_ref=dst, send_sem=ss, recv_sem=rs,
                                        device_id=dev, device_id_type=MESH)


def each(lo, hi, fn):
    def one(s, carry):
        fn(s)
        return carry
    lax.fori_loop(lo, hi, one, 0)


class Moves:
    def __init__(self, prows, pcols, w_ref, c_buf, d_buf, q_buf, p_buf, loc_sem, sems):
        self.prows, self.pcols = prows, pcols
        self.row, self.col = lax.axis_index("prow"), lax.axis_index("pcol")
        self.core = lax.rem(self.col, 2)
        self.w, self.c, self.d, self.q, self.p = w_ref, c_buf, d_buf, q_buf, p_buf
        self.loc = loc_sem
        (self.c_send, self.c_recv, self.cz_send, self.cz_recv,
         self.ds_send, self.ds_recv, self.dz_send, self.dz_recv, self.da_send, self.da_recv,
         self.qs_send, self.qs_recv, self.qa_send, self.qa_recv,
         self.ps_send, self.ps_recv, self.pa_send, self.pa_recv, self.px_send, self.px_recv) = sems
        self.root = jnp.logical_and(self.row == 0, self.col == 0)
        self.passer = self.col == jnp.where(self.row == 0, 1, 0)
        self.pass_hi = jnp.where(self.row == 0, pcols - 1, pcols)
        self.has_q = self.col != 0
        self.has_p = self.row != 0

    def up(self, s):
        return lax.rem(self.row + jnp.where(self.core == 0, s, self.prows - s), self.prows)

    def along(self, s):
        return lax.rem(self.col + s, self.pcols)

    def same_core(self, s):
        return lax.rem(self.col + jnp.where(self.core == 0, 2 * s, self.pcols - 2 * s), self.pcols)

    def ready(self):
        barrier = pltpu.get_barrier_semaphore()

        def tell(dev):
            pl.semaphore_signal(barrier, inc=1, device_id=dev, device_id_type=MESH)
        each(1, self.prows, lambda s: tell({"prow": self.up(s)}))

        @pl.when(self.has_p)
        def _():
            each(1, self.pcols, lambda s: tell({"pcol": self.along(s)}))

        @pl.when(jnp.logical_and(self.row == 0, self.col == 1))
        def _():
            tell({"pcol": 0})

        @pl.when(jnp.logical_and(self.row == 0, self.col > 1))
        def _():
            tell({"pcol": 1})
        zero_row = jnp.where(self.col == 0, 1, jnp.where(self.col == 1, self.pcols - 2, 0))
        pl.semaphore_wait(barrier, self.prows - 1 + jnp.where(self.has_p, self.pcols - 1, zero_row))

    def corner(self, ref, half):
        return ref.at[pl.ds(64 * half, 64), pl.ds(0, TB)]

    def part(self, ref, i, part):
        n = HB // self.prows
        top = pl.ds(pl.multiple_of(i * n, n), n)
        low = pl.multiple_of((i // 2) * n, n)
        side = pl.ds(pl.multiple_of(lax.rem(i, 2) * HB, HB), HB)
        if part == 0:
            return ref.at[top, pl.ds(0, HB)]
        if part in (1, 3):
            return ref.at[top, pl.ds(HB + TB * (part // 2), TB)]
        return ref.at[pl.ds(HB + TB * (part // 2 - 1) + low, n), side]

    def corner_out(self, half, s):
        return rcopy(self.corner(self.w, half), self.corner(self.c, half), self.c_send.at[half, s], self.c_recv.at[half],
                     {"prow": self.up(s)})

    def corner_side(self, half):
        return rcopy(self.corner(self.w, half), self.corner(self.c, half), self.cz_send.at[half, 0], self.cz_recv.at[half],
                     {"pcol": 1})

    def corner_on(self, half, s):
        piece = self.corner(self.c, half)
        return rcopy(piece, piece, self.cz_send.at[half, s], self.cz_recv.at[half], {"pcol": self.along(s)})

    def d_out(self, part, s):
        return rcopy(self.part(self.w, self.up(s), part), self.part(self.d, self.up(s), part),
                     self.ds_send.at[part, s], self.ds_recv.at[part], {"prow": self.up(s)})

    def d_side(self, part):
        return rcopy(self.part(self.w, 0, part), self.part(self.d, 0, part),
                     self.dz_send.at[part, 0], self.dz_recv.at[part], {"pcol": 1})

    def d_on(self, part, s):
        piece = self.part(self.d, self.row, part)
        return rcopy(piece, piece, self.dz_send.at[part, s], self.dz_recv.at[part], {"pcol": self.along(s)})

    def d_share(self, part, s):
        piece = self.part(self.d, self.row, part)
        return rcopy(piece, piece, self.da_send.at[part, s], self.da_recv.at[part, self.row], {"prow": self.up(s)})

    def d_from(self, part, s):
        o = self.up(s)
        piece = self.part(self.d, o, part)
        return rcopy(piece, piece, self.da_send.at[part, s], self.da_recv.at[part, o], {"prow": o})

    def own(self, i):
        if i < 2:
            return pltpu.make_async_copy(self.corner(self.w, i), self.corner(self.c, i), self.loc.at[i])
        if i < 2 + PARTS:
            return pltpu.make_async_copy(self.part(self.w, 0, i - 2), self.part(self.d, 0, i - 2), self.loc.at[i])
        if i == OWN_Q:
            return pltpu.make_async_copy(self.q_piece(self.w, 0), self.q_piece(self.q, 0), self.loc.at[i])
        return pltpu.make_async_copy(self.p_piece(self.w, 0), self.p_piece(self.p, 0), self.loc.at[i])

    def q_piece(self, ref, i):
        n = NB // self.prows
        return ref.at[pl.ds(pl.multiple_of(i * n, n), n), :]

    def q_out(self, s):
        o = self.up(s)
        return rcopy(self.q_piece(self.w, o), self.q_piece(self.q, o), self.qs_send.at[s], self.qs_recv, {"prow": o})

    def q_shares(self, fn):
        first = jnp.where(self.row == 0, self.prows, jnp.where(self.core == 0, self.prows - self.row, self.row))
        each(1, first, lambda s: fn(self.q_share(s)))
        each(first + 1, self.prows, lambda s: fn(self.q_share(s)))

    def q_share(self, s):
        piece = self.q_piece(self.q, self.row)
        return rcopy(piece, piece, self.qa_send.at[s], self.qa_recv.at[self.row], {"prow": self.up(s)})

    def q_from(self, s):
        o = self.up(s)
        piece = self.q_piece(self.q, o)
        return rcopy(piece, piece, self.qa_send.at[s], self.qa_recv.at[o], {"prow": o})

    def p_piece(self, ref, c):
        n = NB // self.pcols
        at = lax.rem(c, 2) * HB + (c // 2) * n
        return ref.at[pl.ds(pl.multiple_of(at, n), n), :]

    def p_half(self, h):
        return self.p.at[pl.ds(pl.multiple_of(h * HB, HB), HB), :]

    def p_out(self, s):
        o = self.along(s)
        return rcopy(self.p_piece(self.w, o), self.p_piece(self.p, o), self.ps_send.at[s], self.ps_recv, {"pcol": o})

    def p_share(self, s):
        piece = self.p_piece(self.p, self.col)
        return rcopy(piece, piece, self.pa_send.at[s], self.pa_recv.at[self.col // 2], {"pcol": self.same_core(s)})

    def p_from(self, s):
        o = self.same_core(s)
        piece = self.p_piece(self.p, o)
        return rcopy(piece, piece, self.pa_send.at[s], self.pa_recv.at[o // 2], {"pcol": o})

    def p_whole(self):
        return rcopy(self.w, self.p, self.px_send, self.px_recv, {"pcol": 1})

    def p_swap(self):
        mine = self.p_half(self.core)
        return rcopy(mine, mine, self.px_send, self.px_recv, {"pcol": self.col + 1 - 2 * self.core})

    def p_swapped(self):
        other = self.p_half(1 - self.core)
        return rcopy(other, other, self.px_send, self.px_recv, {"pcol": self.col + 1 - 2 * self.core})

    def start(self):
        @pl.when(self.root)
        def _():
            self.root_part(0)
            for half in range(2):
                each(1, self.prows, lambda s: self.corner_out(half, s).start())
                self.corner_side(half).start()
                self.own(half).start()
            for part in range(1, PARTS):
                self.root_part(part)

        @pl.when(jnp.logical_and(self.row == 0, self.col > 1))
        def _():
            self.send_q()

        @pl.when(self.passer)
        def _():
            self.pass_part(0)
            for half in range(2):
                @pl.when(self.has_p)
                def _():
                    self.corner_out(half, 0).wait_recv()

                @pl.when(jnp.logical_not(self.has_p))
                def _():
                    self.corner_side(half).wait_recv()
                each(1, self.pass_hi, lambda s: self.corner_on(half, s).start())

    def root_part(self, part):
        each(1, self.prows, lambda s: self.d_out(part, s).start())
        self.d_side(part).start()
        self.own(2 + part).start()

    def pass_part(self, part):
        @pl.when(self.has_p)
        def _():
            self.d_out(part, 0).wait_recv()

        @pl.when(jnp.logical_not(self.has_p))
        def _():
            self.d_side(part).wait_recv()
        each(1, self.pass_hi, lambda s: self.d_on(part, s).start())

    def pass_next(self):
        @pl.when(self.passer)
        def _():
            for part in range(1, 3):
                self.pass_part(part)

            @pl.when(self.has_p)
            def _():
                each(2, self.pcols, lambda s: self.p_out(s).start())
                self.own(OWN_P).start()

    def pass_rest(self):
        @pl.when(self.passer)
        def _():
            for part in range(3, PARTS):
                self.pass_part(part)

            @pl.when(self.has_p)
            def _():
                self.p_whole().start()

            @pl.when(jnp.logical_not(self.has_p))
            def _():
                self.send_q()

    def send_q(self):
        each(1, self.prows, lambda s: self.q_out(s).start())
        self.own(OWN_Q).start()

    def wait_corner(self, half):
        @pl.when(self.root)
        def _():
            self.own(half).wait()

        @pl.when(jnp.logical_not(jnp.logical_or(self.root, self.passer)))
        def _():
            self.corner_on(half, 0).wait_recv()

    def share_d(self, parts):
        for part in parts:
            @pl.when(self.root)
            def _():
                self.own(2 + part).wait()

            @pl.when(jnp.logical_not(jnp.logical_or(self.root, self.passer)))
            def _():
                self.d_on(part, 0).wait_recv()
            each(1, self.prows, lambda s: self.d_share(part, s).start())

    def get_d(self, part):
        each(1, self.prows, lambda s: self.d_from(part, s).wait_recv())

    def share_q(self):
        @pl.when(self.has_q)
        def _():
            @pl.when(self.row == 0)
            def _():
                self.own(OWN_Q).wait()

            @pl.when(self.row != 0)
            def _():
                self.q_out(0).wait_recv()
            self.q_shares(lambda copy: copy.start())

    def get_q(self, q_ref):
        @pl.when(self.row == 0)
        def _():
            q_ref[...] = self.w[...].astype(F32)

        @pl.when(self.row != 0)
        def _():
            each(1, self.prows, lambda s: self.q_from(s).wait_recv())
            q_ref[...] = self.q[...].astype(F32)

    def share_p(self):
        @pl.when(self.has_p)
        def _():
            @pl.when(self.col == 1)
            def _():
                self.p_whole().wait_recv()

            @pl.when(self.col > 1)
            def _():
                self.p_out(0).wait_recv()
            @pl.when(self.col == 0)
            def _():
                self.own(OWN_P).wait()
            self.p_shares(lambda copy: copy.start())

    def p_shares(self, fn):
        chips = self.pcols // 2
        mine = self.col // 2
        skip = jnp.where(mine == 0, chips, jnp.where(self.core == 0, chips - mine, mine))
        each(1, skip, lambda s: fn(self.p_share(s)))
        each(skip + 1, chips, lambda s: fn(self.p_share(s)))

    def swap_p(self):
        @pl.when(self.has_p)
        def _():
            @pl.when(self.col > 1)
            def _():
                each(1, self.pcols // 2, lambda s: self.p_from(s).wait_recv())
                self.p_swap().start()

    def get_p(self, p_ref):
        @pl.when(self.col == 0)
        def _():
            p_ref[...] = self.w[...].astype(F32)

        @pl.when(self.col > 1)
        def _():
            self.p_swapped().wait_recv()

        @pl.when(self.col != 0)
        def _():
            p_ref[...] = self.p[...].astype(F32)

    def finish(self):
        @pl.when(self.root)
        def _():
            for half in range(2):
                each(1, self.prows, lambda s: self.corner_out(half, s).wait_send())
                self.corner_side(half).wait_send()
            for part in range(PARTS):
                each(1, self.prows, lambda s: self.d_out(part, s).wait_send())
                self.d_side(part).wait_send()

        @pl.when(self.passer)
        def _():
            for half in range(2):
                each(1, self.pass_hi, lambda s: self.corner_on(half, s).wait_send())
            for part in range(PARTS):
                each(1, self.pass_hi, lambda s: self.d_on(part, s).wait_send())

            @pl.when(self.has_p)
            def _():
                each(2, self.pcols, lambda s: self.p_out(s).wait_send())
        for part in range(PARTS):
            each(1, self.prows, lambda s: self.d_share(part, s).wait_send())

        @pl.when(self.has_q)
        def _():
            @pl.when(self.row == 0)
            def _():
                each(1, self.prows, lambda s: self.q_out(s).wait_send())
            self.q_shares(lambda copy: copy.wait_send())

        @pl.when(self.has_p)
        def _():
            self.p_shares(lambda copy: copy.wait_send())

            @pl.when(self.col == 0)
            def _():
                self.p_whole().wait_send()

            @pl.when(self.col > 1)
            def _():
                self.p_swap().wait_send()


def step_kernel(prows, pcols, w_hbm, o_ref, w_ref, a_ref, q_ref, p_ref, li_ref, ui_ref, ub_ref, lb_ref,
                c_buf, d_buf, q_buf, p_buf, loc_sem, *sems):
    mv = Moves(prows, pcols, w_ref, c_buf, d_buf, q_buf, p_buf, loc_sem, sems)
    load = pltpu.make_async_copy(w_hbm, w_ref, loc_sem.at[OWN_P + 1])
    load.start()
    mv.ready()
    load.wait()
    mv.start()
    mv.share_d([0])
    mv.wait_corner(0)
    a_ref[0:64, 0:TB] = c_buf[0:64, :].astype(F32)

    def tile_step(k, carry):
        at = pl.ds(pl.multiple_of(k * TB, TB), TB)
        upper = pl.ds(pl.multiple_of(k * TB, 64), 64)
        lower = pl.ds(pl.multiple_of(k * TB + 64, 64), 64)
        top = a_ref[upper, at]
        t0, b0 = leaf(top, 0)

        @pl.when(k == 0)
        def _():
            mv.wait_corner(1)
            a_ref[64:TB, 0:TB] = c_buf[64:TB, :].astype(F32)
            mv.pass_next()

        @pl.when(k == 1)
        def _():
            mv.share_d([3, 4])
            mv.share_q()
            mv.share_p()

        packed, linv, uinv = second_half(t0, b0, top, a_ref[lower, at])
        a_ref[at, at] = packed
        li_ref[k] = linv
        ui_ref[k] = uinv

        @pl.when(k == 0)
        def _():
            mv.pass_rest()
            mv.share_d([1, 2])
            mv.get_d(0)
            a_ref[0:TB, TB:HB] = d_buf[0:TB, TB:HB].astype(F32)
            a_ref[TB:HB, 0:HB] = d_buf[TB:HB, 0:HB].astype(F32)
            strip_update(a_ref, li_ref, ui_ref, 1)

        @pl.when(k == 1)
        def _():
            mv.get_d(1)
            mv.get_d(2)
            a_ref[0:HB, HB:HB + TB] = d_buf[0:HB, HB:HB + TB].astype(F32)
            a_ref[HB:HB + TB, 0:HB + TB] = d_buf[HB:HB + TB, 0:HB + TB].astype(F32)
            strip_update(a_ref, li_ref, ui_ref, 2)

        @pl.when(k == 2)
        def _():
            mv.get_d(3)
            mv.get_d(4)
            mv.swap_p()
            a_ref[0:HB + TB, HB + TB:NB] = d_buf[0:HB + TB, HB + TB:NB].astype(F32)
            a_ref[HB + TB:NB, :] = d_buf[HB + TB:NB, :].astype(F32)
            strip_update(a_ref, li_ref, ui_ref, 3)
        return carry

    lax.fori_loop(0, 4, tile_step, 0)

    @pl.when(mv.has_q)
    def _():
        mv.get_q(q_ref)

    @pl.when(mv.has_p)
    def _():
        mv.get_p(p_ref)

    @pl.when(jnp.logical_and(mv.has_p, mv.has_q))
    def _():
        for j in range(4):
            solve_u(a_ref, li_ref, q_ref, ub_ref, j)
            solve_l(a_ref, ui_ref, p_ref, lb_ref, j)
        o_ref[...] = (w_ref[...].astype(F32) - dot(lb_ref[...], ub_ref[...])).astype(BF)

    @pl.when(jnp.logical_and(jnp.logical_not(mv.has_p), mv.has_q))
    def _():
        for j in range(4):
            solve_u(a_ref, li_ref, q_ref, ub_ref, j)
        o_ref[...] = ub_ref[...]

    @pl.when(jnp.logical_and(mv.has_p, jnp.logical_not(mv.has_q)))
    def _():
        for j in range(4):
            solve_l(a_ref, ui_ref, p_ref, lb_ref, j)
        o_ref[...] = lb_ref[...]

    @pl.when(mv.root)
    def _():
        o_ref[...] = a_ref[...].astype(BF)

    mv.finish()


def per_device(matrix):
    prows, pcols = lax.axis_size("prow"), lax.axis_size("pcol")
    dma = pltpu.SemaphoreType.DMA
    out = pl.pallas_call(
        functools.partial(step_kernel, prows, pcols),
        out_shape=pltpu.VMEM((NB, NB), BF),
        in_specs=[pl.BlockSpec(memory_space=pl.ANY)],
        out_specs=pl.BlockSpec(memory_space=pltpu.VMEM),
        scratch_shapes=[
            pltpu.VMEM((NB, NB), BF),
            pltpu.VMEM((NB, NB), F32), pltpu.VMEM((NB, NB), F32), pltpu.VMEM((NB, NB), F32),
            pltpu.VMEM((4, TB, TB), F32), pltpu.VMEM((4, TB, TB), F32),
            pltpu.VMEM((NB, NB), BF), pltpu.VMEM((NB, NB), BF),
            pltpu.VMEM((TB, TB), BF), pltpu.VMEM((NB, NB), BF), pltpu.VMEM((NB, NB), BF), pltpu.VMEM((NB, NB), BF),
            dma((5 + PARTS,)),
            dma((2, prows)), dma((2,)), dma((2, pcols)), dma((2,)),
            dma((PARTS, prows)), dma((PARTS,)), dma((PARTS, pcols)), dma((PARTS,)), dma((PARTS, prows)), dma((PARTS, prows)),
            dma((prows,)), dma, dma((prows,)), dma((prows,)),
            dma((pcols,)), dma, dma((pcols // 2,)), dma((pcols // 2,)), dma, dma,
        ],
        compiler_params=pltpu.CompilerParams(collective_id=0, has_side_effects=True),
    )(matrix.reshape(NB, NB))
    return out.reshape(matrix.shape)


def solution(mesh):
    placed = P(None, "prow", None, "pcol")
    return jax.shard_map(per_device, mesh=mesh, in_specs=(placed,), out_specs=placed, check_vma=False)
```
